32 devices in a mesh: tile: 8 (over y, x, core), member: 4 (over z).
Axes of the slice: x: 2, y: 2, z: 4, core: 2. Of those that a mesh axis runs over, the one named last changes fastest.
Arguments:
- hx: bfloat16 [512, 32768], P('member', 'tile'), may hold values from -6 to 6
- obs_value: bfloat16 [32768], P('tile'), may hold values from -8 to 8
- obs_rinv: bfloat16 [32768], P('tile'), may hold values from 0.29882812 to 4
- obs_index: int32 [32, 1024], P('tile'), may hold values from 512 to 5631, as said below
- loc_weight: float32 [32, 1024], P(('tile', 'member')), may hold values from 0.05 to 1
- state: bfloat16 [512, 131072], P('member', 'tile'), may hold values from -6 to 6
Outputs:
- analysis: bfloat16 [512, 131072], P('member', 'tile')
The draws below stay inside these ranges and needn't reach their ends.
Inputs may be any that keep to these rules, and one draw needn't show every extreme that they name: `obs_index`: row p lists 1024 distinct positions in the pool of tile p // 4: positions 0 .. 1023 are the last 1024 observations of the tile before it, the next 4096 the tile's own, the last 1024 the first observations of the tile after it; the tiles form a closed band. All positions of a row lie within 2048 consecutive positions.
All inputs are finite; a program needn't handle non-finite values.
Results may differ from the reference program's by a relative error of at most 0.012.
The reference program's roundings to bfloat16 on the way (of `obs_block`, `scaled`, `transform` and `state_pert`) count: a program that leaves them out, or rounds other values in their place, can miss the bound.
Values may be sent and summed in bfloat16 or wider, within the bound.
No kernel may reach another device: no remote copies, remote signals or barrier semaphores. Data moves between devices by JAX's collectives and lax.ppermute only.
A program may use at most 64 MiB of HBM per device.

```python
import math
import jax
import jax.numpy as jnp
from jax import lax

ENS = 512
NOBS_DEV = 4096
LOC = 1024
CELLS_DEV = 16384
NS_ITERS = 3
NOBS = 32768
CELLS = 131072
PATCHES = 32
N_MEMBER = 4


def draw_obs_index(key, part):
    patch_pos = jnp.arange(PATCHES, dtype=jnp.int32) % N_MEMBER
    starts = (2 * patch_pos + 1) * NOBS_DEV // (2 * N_MEMBER)
    keys = jax.random.split(key, PATCHES)
    offsets = jax.vmap(lambda single: jax.random.permutation(single, 2 * LOC)[:LOC])(keys)
    return (starts[:, None] + offsets).astype(jnp.int32)


def shard_levels(rng, extent, cuts, smallest, top_value):
    loudness, own = 1.0, jax.random.fold_in(rng, 6)
    for dim, blocks in cuts:
        heights = jnp.exp(jax.random.uniform(jax.random.fold_in(own, dim), (blocks,), jnp.float32, smallest / len(cuts), top_value / len(cuts)))
        loudness = loudness * jnp.repeat(heights, extent[dim] // blocks).reshape([-1 if axis == dim else 1 for axis in range(len(extent))])
    return loudness


def noise(key, shape, deviation, most, cuts=(), kind=jnp.bfloat16):
    result = deviation * jax.random.normal(key, shape, jnp.float32)
    if cuts:
        result = result * shard_levels(key, shape, cuts, -0.22, 0.18)
    return jnp.clip(result, -most, most).astype(kind)


def setup_inputs(seed: int = 0) -> dict:
    splits = jax.random.split(jax.random.key(seed), 7)
    hx = noise(splits[0], (ENS, NOBS), 1.0, 6.0, ((0, 4), (1, 8)))
    obs_value = noise(splits[1], (NOBS,), 1.5, 8.0, ((0, 8),))
    obs_rinv = jnp.clip(jnp.exp(math.log(4.0) - 2.594181 * jax.random.uniform(splits[2], (NOBS,), jnp.float32) ** shard_levels(splits[2], (NOBS,), ((0, 8),), -0.2, 0.2)), 0.29882812, 4.0).astype(jnp.bfloat16)
    obs_index = draw_obs_index(jax.random.fold_in(splits[6], 71), 0)
    loc_weight = jnp.clip(jnp.exp(math.log(1.0) - 2.9957323 * jax.random.uniform(splits[4], (PATCHES, LOC), jnp.float32) ** shard_levels(splits[4], (PATCHES, LOC), ((0, 32),), -0.2, 0.2)), 0.05, 1.0)
    state = noise(splits[5], (ENS, CELLS), 1.0, 6.0, ((0, 4), (1, 8)))
    return {"hx": hx, "obs_value": obs_value, "obs_rinv": obs_rinv, "obs_index": obs_index, "loc_weight": loc_weight, "state": state}


def product_f32(left, right, dims):
    return lax.dot_general(left.astype(jnp.float32), right.astype(jnp.float32), (dims, ((), ())), precision=lax.Precision.HIGHEST, preferred_element_type=jnp.float32)

def analysis(obs_block, obs_pair, loc_row):
    members = obs_block.shape[0]
    block_f = obs_block.astype(jnp.float32)
    obs_mean = lax.optimization_barrier(jnp.mean(block_f, axis=0))
    obs_root = jnp.sqrt(obs_pair[1].astype(jnp.float32) * loc_row)
    scaled = ((block_f - obs_mean) * obs_root).astype(jnp.bfloat16)
    innovation = (obs_pair[0].astype(jnp.float32) - obs_mean) * obs_root
    gram_matrix = product_f32(scaled, scaled, ((1,), (1,)))
    identity = jnp.eye(members, dtype=jnp.float32)
    system = gram_matrix + (members - 1.0) * identity
    projection = jnp.dot(scaled.astype(jnp.float32), innovation, precision=lax.Precision.HIGHEST)
    norm_a = jnp.sqrt(jnp.sum(system * system))
    upper_iter = system / norm_a
    lower_iter = identity
    for sweep in range(NS_ITERS):
        upper_b = upper_iter.astype(jnp.bfloat16)
        lower_b = lower_iter.astype(jnp.bfloat16)
        product = product_f32(lower_b, upper_b, ((1,), (0,)))
        half_step = (1.5 * identity - 0.5 * product).astype(jnp.bfloat16)
        if sweep + 1 < NS_ITERS:
            upper_iter = product_f32(upper_b, half_step, ((1,), (0,)))
        lower_iter = product_f32(half_step, lower_b, ((1,), (0,)))
    invroot = lower_iter / jnp.sqrt(norm_a)
    inner_w = jnp.dot(invroot, projection, precision=lax.Precision.HIGHEST)
    mean_w = jnp.dot(invroot, inner_w, precision=lax.Precision.HIGHEST)
    transform = jnp.sqrt(members - 1.0) * invroot + mean_w[:, None]
    return transform.astype(jnp.bfloat16)

def transform_state(transform, state_block):
    block_f = state_block.astype(jnp.float32)
    state_mean = lax.optimization_barrier(jnp.mean(block_f, axis=0))
    state_pert = (block_f - state_mean).astype(jnp.bfloat16)
    combined = product_f32(transform, state_pert, ((0,), (0,)))
    return (state_mean + combined).astype(jnp.bfloat16)

def reference(hx, obs_value, obs_rinv, obs_index, loc_weight, state):
    obs_total = hx.shape[1]
    patch_cells = CELLS_DEV // N_MEMBER

    def one_patch(patch):
        tile_pos = patch // N_MEMBER
        index_row = lax.dynamic_index_in_dim(obs_index, patch, 0, keepdims=False)
        global_cols = ((tile_pos * NOBS_DEV - LOC + index_row) % obs_total).astype(jnp.int32)
        obs_block = jnp.take(hx, global_cols, axis=1)
        obs_pair = jnp.stack([jnp.take(obs_value, global_cols), jnp.take(obs_rinv, global_cols)])
        loc_row = lax.dynamic_index_in_dim(loc_weight, patch, 0, keepdims=False)
        transform = analysis(obs_block, obs_pair, loc_row)
        start = (patch * patch_cells).astype(jnp.int32)
        state_block = lax.dynamic_slice_in_dim(state, start, patch_cells, 1)
        return transform_state(transform, state_block)
    blocks = lax.map(one_patch, jnp.arange(PATCHES, dtype=jnp.int32))
    return jnp.transpose(blocks, (1, 0, 2)).reshape(ENS, PATCHES * patch_cells)
```

```python
import functools

import jax
import jax.numpy as jnp
from jax import lax
from jax.experimental import pallas as pl
from jax.experimental.pallas import tpu as pltpu
from jax.sharding import PartitionSpec as P

LOC = 1024
NS_ITERS = 3
LANES = 128
WINDOW = 2 * LOC
CHUNKS = 2
BLOCK = 512


def partners(count, step):
    return [(i, i ^ step) for i in range(count)]


def swap(block, step):
    return lax.ppermute(block, "member", partners(lax.axis_size("member"), step))


def split_kernel(pos_ref, *refs):
    half = len(refs) // 2
    for source, target in zip(refs[:half], refs[half:]):
        target[...] = source[...]


def split_state(position, state, chunk, count):
    rows, total = state.shape
    width = total // (count * CHUNKS)
    specs = [
        pl.BlockSpec(
            (rows, width),
            functools.partial(lambda i, pos, step: (0, (pos[0] ^ step) * CHUNKS + chunk), step=step),
        )
        for step in range(1, count)
    ]
    outs = [pl.BlockSpec((rows, width), lambda i, pos: (0, 0)) for _ in range(1, count)]
    return pl.pallas_call(
        split_kernel,
        grid_spec=pltpu.PrefetchScalarGridSpec(
            num_scalar_prefetch=1, grid=(1,), in_specs=specs, out_specs=outs
        ),
        out_shape=[jax.ShapeDtypeStruct((rows, width), state.dtype)] * (count - 1),
        cost_estimate=pl.CostEstimate(
            flops=0, transcendentals=0, bytes_accessed=4 * (count - 1) * rows * width
        ),
    )(position, *[state] * (count - 1))


def pick_kernel(pos_ref, start_ref, index_ref, own_ref, low_ref, high_ref, out_ref, pair_ref, pool):
    step = pl.program_id(0)
    rows = own_ref.shape[0]
    own = own_ref.shape[1]
    span = WINDOW + LANES

    @pl.when(step == 0)
    def _():
        pool[:, :LOC] = low_ref[...]
        pool[:, LOC : LOC + own] = own_ref[...]
        pool[:, LOC + own :] = high_ref[...]

    start = pl.multiple_of(start_ref[pos_ref[0] ^ step], LANES)
    relative = index_ref[0] - start
    window = pool[:, pl.ds(start, span)]
    half = LOC // 4
    for part in range(4):
        where = relative[:, part * half : (part + 1) * half]
        hot = lax.broadcasted_iota(jnp.int32, (span, half), 0) == where
        hot = jnp.where(hot, 1.0, 0.0).astype(jnp.bfloat16)
        picked = jnp.dot(window, hot, preferred_element_type=jnp.float32)
        picked = picked.astype(jnp.bfloat16)
        out_ref[0, :, part * half : (part + 1) * half] = picked[: out_ref.shape[1]]

        @pl.when(step == 0)
        def _():
            pair_ref[:, part * half : (part + 1) * half] = picked[out_ref.shape[1] :]


def pick(position, starts, index, own, low, high, members):
    count = index.shape[0]
    rows, width = own.shape
    whole = lambda shape: pl.BlockSpec(shape, lambda i, pos, start: (0,) * len(shape))
    return pl.pallas_call(
        pick_kernel,
        grid_spec=pltpu.PrefetchScalarGridSpec(
            num_scalar_prefetch=2,
            grid=(count,),
            in_specs=[
                pl.BlockSpec((1, 1, LOC), lambda i, pos, start: (pos[0] ^ i, 0, 0)),
                whole(own.shape),
                whole(low.shape),
                whole(high.shape),
            ],
            out_specs=[
                pl.BlockSpec((1, members, LOC), lambda i, pos, start: (i, 0, 0)),
                whole((rows - members, LOC)),
            ],
            scratch_shapes=[pltpu.VMEM((rows, width + 2 * LOC), jnp.bfloat16)],
        ),
        out_shape=[
            jax.ShapeDtypeStruct((count, members, LOC), jnp.bfloat16),
            jax.ShapeDtypeStruct((rows - members, LOC), jnp.bfloat16),
        ],
        cost_estimate=pl.CostEstimate(
            flops=2 * count * rows * (WINDOW + LANES) * LOC,
            transcendentals=0,
            bytes_accessed=2 * rows * width + 2 * count * rows * LOC,
        ),
    )(position, starts, index.reshape(count, 1, LOC), own, low, high)


def update_kernel(count, aliased, pos_ref, transform_ref, *refs):
    blocks = refs[:count]
    outs = refs[count + aliased : 2 * count + aliased]
    pert = refs[-1]
    rows = blocks[0].shape[0]
    values = [block[...].astype(jnp.float32) for block in blocks]
    total = jnp.sum(values[0], axis=0, keepdims=True)
    for value in values[1:]:
        total += jnp.sum(value, axis=0, keepdims=True)
    mean = total / (count * rows)
    for k, value in enumerate(values):
        pert[k * rows : (k + 1) * rows, :] = (value - mean).astype(jnp.bfloat16)
    combined = jnp.dot(transform_ref[...], pert[...], preferred_element_type=jnp.float32)
    result = (mean + combined).astype(jnp.bfloat16)
    for k in range(count):
        outs[k][...] = result[k * rows : (k + 1) * rows]


def update_state(position, transform, state, received, chunk, buffer):
    rows, total = state.shape
    count = len(received) + 1
    members = transform.shape[0]
    width = received[0].shape[1]
    block = min(BLOCK, width)
    per = width // block
    own = pl.BlockSpec((rows, block), lambda i, pos: (0, (pos[0] * CHUNKS + chunk) * per + i))
    plain = pl.BlockSpec((rows, block), lambda i, pos: (0, i))
    aliased = 0 if buffer is None else 1
    extra = [] if buffer is None else [pl.BlockSpec(memory_space=pl.ANY)]
    return pl.pallas_call(
        functools.partial(update_kernel, count, aliased),
        grid_spec=pltpu.PrefetchScalarGridSpec(
            num_scalar_prefetch=1,
            grid=(per,),
            in_specs=[pl.BlockSpec((members, members), lambda i, pos: (0, 0)), own]
            + [plain] * (count - 1)
            + extra,
            out_specs=[own] + [plain] * (count - 1),
            scratch_shapes=[pltpu.VMEM((members, block), jnp.bfloat16)],
        ),
        out_shape=[jax.ShapeDtypeStruct((rows, total), state.dtype)]
        + [jax.ShapeDtypeStruct((rows, width), state.dtype)] * (count - 1),
        input_output_aliases={} if buffer is None else {2 + count: 0},
        cost_estimate=pl.CostEstimate(
            flops=2 * members * members * width,
            transcendentals=0,
            bytes_accessed=4 * members * width + 2 * members * members,
        ),
    )(position, transform, state, *received, *([] if buffer is None else [buffer]))


def place_kernel(count, pos_ref, *refs):
    pieces, out = refs[:count], refs[-1]
    for step, piece in enumerate(pieces, 1):

        @pl.when(pl.program_id(0) == step - 1)
        def _():
            out[...] = piece[...]


def place(position, buffer, pieces, chunk):
    rows, width = pieces[0].shape
    count = len(pieces)
    return pl.pallas_call(
        functools.partial(place_kernel, count),
        grid_spec=pltpu.PrefetchScalarGridSpec(
            num_scalar_prefetch=1,
            grid=(count,),
            in_specs=[pl.BlockSpec((rows, width), lambda i, pos: (0, 0))] * count
            + [pl.BlockSpec(memory_space=pl.ANY)],
            out_specs=pl.BlockSpec(
                (rows, width), lambda i, pos: (0, (pos[0] ^ (i + 1)) * CHUNKS + chunk)
            ),
        ),
        out_shape=jax.ShapeDtypeStruct(buffer.shape, buffer.dtype),
        input_output_aliases={count + 1: 0},
        cost_estimate=pl.CostEstimate(
            flops=0, transcendentals=0, bytes_accessed=4 * count * rows * width
        ),
    )(position, *pieces, buffer)


def product(left, right, dims):
    return lax.dot_general(left, right, (dims, ((), ())), preferred_element_type=jnp.float32)


def analysis(obs_block, obs_pair, loc_row):
    members = obs_block.shape[0]
    block_f = obs_block.astype(jnp.float32)
    obs_mean = jnp.mean(block_f, axis=0)
    obs_root = jnp.sqrt(obs_pair[1].astype(jnp.float32) * loc_row)
    scaled = ((block_f - obs_mean) * obs_root).astype(jnp.bfloat16)
    innovation = (obs_pair[0].astype(jnp.float32) - obs_mean) * obs_root
    gram_matrix = product(scaled, scaled, ((1,), (1,)))
    identity = jnp.eye(members, dtype=jnp.float32)
    system = gram_matrix + (members - 1.0) * identity
    projection = jnp.dot(scaled.astype(jnp.float32), innovation, precision=lax.Precision.HIGHEST)
    norm_a = jnp.sqrt(jnp.sum(system * system))
    upper_iter = system / norm_a
    lower_iter = identity
    for sweep in range(NS_ITERS):
        upper_b = upper_iter.astype(jnp.bfloat16)
        lower_b = lower_iter.astype(jnp.bfloat16)
        half_step = (1.5 * identity - 0.5 * product(lower_b, upper_b, ((1,), (0,)))).astype(
            jnp.bfloat16
        )
        if sweep + 1 < NS_ITERS:
            upper_iter = product(upper_b, half_step, ((1,), (0,)))
        lower_iter = product(half_step, lower_b, ((1,), (0,)))
    invroot = lower_iter / jnp.sqrt(norm_a)
    inner_w = jnp.dot(invroot, projection, precision=lax.Precision.HIGHEST)
    mean_w = jnp.dot(invroot, inner_w, precision=lax.Precision.HIGHEST)
    transform = jnp.sqrt(members - 1.0) * invroot + mean_w[:, None]
    return transform.astype(jnp.bfloat16).T


def shift_tiles(block, step):
    count = lax.axis_size("tile")
    return lax.ppermute(block, "tile", [(i, (i + step) % count) for i in range(count)])


def on_device(hx, obs_value, obs_rinv, obs_index, loc_weight, state):
    rows = hx.shape[0]
    count = lax.axis_size("member")
    position = lax.axis_index("member").astype(jnp.int32).reshape(1)

    first = split_state(position, state, 0, count)
    arrived = [[swap(piece, step) for step, piece in enumerate(first, 1)]]

    pad = jnp.zeros((14, hx.shape[1]), hx.dtype)
    stacked = jnp.concatenate([hx, obs_value[None], obs_rinv[None], pad], axis=0)
    low = shift_tiles(stacked[:, -LOC:], 1)
    high = shift_tiles(stacked[:, :LOC], -1)
    limit = hx.shape[1] - WINDOW + 2 * LOC - LANES
    starts = jnp.minimum(jnp.min(obs_index, axis=1) // LANES * LANES, limit)
    picked, obs_pair = pick(position, starts, obs_index, stacked, low, high, rows)
    received = [picked[0]] + [swap(picked[step], step) for step in range(1, count)]

    for chunk in range(1, CHUNKS):
        pieces = split_state(position, state, chunk, count)
        arrived.append([swap(piece, step) for step, piece in enumerate(pieces, 1)])

    transform = analysis(jnp.concatenate(received, axis=0), obs_pair, loc_weight[0])

    buffer, returned = None, []
    for chunk in range(CHUNKS):
        buffer, *others = update_state(position, transform, state, arrived[chunk], chunk, buffer)
        returned.append([swap(piece, step) for step, piece in enumerate(others, 1)])
    for chunk in range(CHUNKS):
        buffer = place(position, buffer, returned[chunk], chunk)
    return buffer


def solution(mesh):
    in_specs = (
        P("member", "tile"),
        P("tile"),
        P("tile"),
        P("tile", None),
        P(("tile", "member"), None),
        P("member", "tile"),
    )
    out_specs = P("member", "tile")
    return jax.shard_map(
        on_device, mesh=mesh, in_specs=in_specs, out_specs=out_specs, check_vma=False
    )
```

```python
import functools

import jax
import jax.numpy as jnp
from jax import lax
from jax.experimental import pallas as pl
from jax.experimental.pallas import tpu as pltpu
from jax.sharding import PartitionSpec as P


LOC = 1024
NS_ITERS = 3
LANES = 128
WINDOW = 2 * LOC
CHUNKS = 2
BLOCK = 512


def partners(count, step):
    return [(i, i ^ step) for i in range(count)]


def swap(block, step):
    return lax.ppermute(block, "member", partners(lax.axis_size("member"), step))


def cut_kernel(first, pos_ref, state_ref, out_ref, sem):
    width = out_ref.shape[1]
    start = pl.multiple_of(first(pos_ref[0]) * width, LANES)
    copy = pltpu.make_async_copy(state_ref.at[:, pl.ds(start, width)], out_ref, sem)
    copy.start()
    copy.wait()


def cut(position, state, step, chunk, count):
    rows, total = state.shape
    width = total // (count * CHUNKS)
    return pl.pallas_call(
        functools.partial(cut_kernel, lambda pos: (pos ^ step) * CHUNKS + chunk),
        in_specs=[
            pl.BlockSpec(memory_space=pltpu.SMEM),
            pl.BlockSpec(memory_space=pl.ANY),
        ],
        out_specs=pl.BlockSpec(memory_space=pltpu.VMEM),
        scratch_shapes=[pltpu.SemaphoreType.DMA],
        out_shape=jax.ShapeDtypeStruct((rows, width), state.dtype),
        cost_estimate=pl.CostEstimate(
            flops=0, transcendentals=0, bytes_accessed=2 * rows * width
        ),
    )(position, state)


def pick_kernel(pos_ref, start_ref, index_ref, own_ref, low_ref, high_ref, out_ref, pair_ref, pool):
    step = pl.program_id(0)
    own = own_ref.shape[1]
    span = WINDOW + LANES

    @pl.when(step == 0)
    def _():
        pool[:, :LOC] = low_ref[...]
        pool[:, LOC : LOC + own] = own_ref[...]
        pool[:, LOC + own :] = high_ref[...]

    start = pl.multiple_of(start_ref[pos_ref[0] ^ step], LANES)
    relative = index_ref[0] - start
    window = pool[:, pl.ds(start, span)]
    half = LOC // 4
    for part in range(4):
        where = relative[:, part * half : (part + 1) * half]
        hot = lax.broadcasted_iota(jnp.int32, (span, half), 0) == where
        hot = jnp.where(hot, 1.0, 0.0).astype(jnp.bfloat16)
        picked = jnp.dot(window, hot, preferred_element_type=jnp.float32)
        picked = picked.astype(jnp.bfloat16)
        out_ref[0, :, part * half : (part + 1) * half] = picked[: out_ref.shape[1]]

        @pl.when(step == 0)
        def _():
            pair_ref[:, part * half : (part + 1) * half] = picked[out_ref.shape[1] :]


def pick(position, starts, index, own, low, high, members):
    count = index.shape[0]
    rows, width = own.shape
    whole = lambda shape: pl.BlockSpec(shape, lambda i, pos, start: (0,) * len(shape))
    return pl.pallas_call(
        pick_kernel,
        grid_spec=pltpu.PrefetchScalarGridSpec(
            num_scalar_prefetch=2,
            grid=(count,),
            in_specs=[
                pl.BlockSpec((1, 1, LOC), lambda i, pos, start: (pos[0] ^ i, 0, 0)),
                whole(own.shape),
                whole(low.shape),
                whole(high.shape),
            ],
            out_specs=[
                pl.BlockSpec((1, members, LOC), lambda i, pos, start: (i, 0, 0)),
                whole((rows - members, LOC)),
            ],
            scratch_shapes=[pltpu.VMEM((rows, width + 2 * LOC), jnp.bfloat16)],
        ),
        compiler_params=pltpu.CompilerParams(vmem_limit_bytes=20 << 20),
        out_shape=[
            jax.ShapeDtypeStruct((count, members, LOC), jnp.bfloat16),
            jax.ShapeDtypeStruct((rows - members, LOC), jnp.bfloat16),
        ],
        cost_estimate=pl.CostEstimate(
            flops=2 * count * rows * (WINDOW + LANES) * LOC,
            transcendentals=0,
            bytes_accessed=2 * rows * width + 2 * count * rows * LOC,
        ),
    )(position, starts, index.reshape(count, 1, LOC), own, low, high)


def update_kernel(count, aliased, pos_ref, transform_ref, *refs):
    blocks = refs[:count]
    outs = refs[count + aliased : 2 * count + aliased]
    pert = refs[-1]
    rows = blocks[0].shape[0]
    values = [block[...].astype(jnp.float32) for block in blocks]
    total = jnp.sum(values[0], axis=0, keepdims=True)
    for value in values[1:]:
        total += jnp.sum(value, axis=0, keepdims=True)
    mean = total / (count * rows)
    for k, value in enumerate(values):
        pert[k * rows : (k + 1) * rows, :] = (value - mean).astype(jnp.bfloat16)
    combined = jnp.dot(transform_ref[...], pert[...], preferred_element_type=jnp.float32)
    result = (mean + combined).astype(jnp.bfloat16)
    for k in range(count):
        outs[k][...] = result[k * rows : (k + 1) * rows]


def update_state(position, transform, state, received, chunk, buffer):
    rows, total = state.shape
    count = len(received) + 1
    members = transform.shape[0]
    width = received[0].shape[1]
    block = min(BLOCK, width)
    per = width // block
    own = pl.BlockSpec((rows, block), lambda i, pos: (0, (pos[0] * CHUNKS + chunk) * per + i))
    plain = pl.BlockSpec((rows, block), lambda i, pos: (0, i))
    aliased = 0 if buffer is None else 1
    extra = [] if buffer is None else [pl.BlockSpec(memory_space=pl.ANY)]
    return pl.pallas_call(
        functools.partial(update_kernel, count, aliased),
        grid_spec=pltpu.PrefetchScalarGridSpec(
            num_scalar_prefetch=1,
            grid=(per,),
            in_specs=[pl.BlockSpec((members, members), lambda i, pos: (0, 0)), own]
            + [plain] * (count - 1)
            + extra,
            out_specs=[own] + [plain] * (count - 1),
            scratch_shapes=[pltpu.VMEM((members, block), jnp.bfloat16)],
        ),
        out_shape=[jax.ShapeDtypeStruct((rows, total), state.dtype)]
        + [jax.ShapeDtypeStruct((rows, width), state.dtype)] * (count - 1),
        input_output_aliases={} if buffer is None else {2 + count: 0},
        compiler_params=pltpu.CompilerParams(vmem_limit_bytes=16 << 20),
        cost_estimate=pl.CostEstimate(
            flops=2 * members * members * width,
            transcendentals=0,
            bytes_accessed=4 * members * width + 2 * members * members,
        ),
    )(position, transform, state, *received, *([] if buffer is None else [buffer]))


def place_kernel(first, pos_ref, piece_ref, buffer_ref, out_ref, sem):
    width = piece_ref.shape[1]
    start = pl.multiple_of(first(pos_ref[0]) * width, LANES)
    copy = pltpu.make_async_copy(piece_ref, out_ref.at[:, pl.ds(start, width)], sem)
    copy.start()
    copy.wait()


def place(position, buffer, piece, step, chunk):
    rows, width = piece.shape
    return pl.pallas_call(
        functools.partial(place_kernel, lambda pos: (pos ^ step) * CHUNKS + chunk),
        in_specs=[
            pl.BlockSpec(memory_space=pltpu.SMEM),
            pl.BlockSpec(memory_space=pl.ANY),
            pl.BlockSpec(memory_space=pl.ANY),
        ],
        out_specs=pl.BlockSpec(memory_space=pl.ANY),
        scratch_shapes=[pltpu.SemaphoreType.DMA],
        compiler_params=pltpu.CompilerParams(vmem_limit_bytes=1 << 20),
        out_shape=jax.ShapeDtypeStruct(buffer.shape, buffer.dtype),
        input_output_aliases={2: 0},
        cost_estimate=pl.CostEstimate(
            flops=0, transcendentals=0, bytes_accessed=2 * rows * width
        ),
    )(position, piece, buffer)


def product(left, right, dims):
    return lax.dot_general(left, right, (dims, ((), ())), preferred_element_type=jnp.float32)


def analysis(obs_block, obs_pair, loc_row):
    members = obs_block.shape[0]
    block_f = obs_block.astype(jnp.float32)
    obs_mean = jnp.mean(block_f, axis=0)
    obs_root = jnp.sqrt(obs_pair[1].astype(jnp.float32) * loc_row)
    scaled = ((block_f - obs_mean) * obs_root).astype(jnp.bfloat16)
    innovation = (obs_pair[0].astype(jnp.float32) - obs_mean) * obs_root
    gram_matrix = product(scaled, scaled, ((1,), (1,)))
    identity = jnp.eye(members, dtype=jnp.float32)
    system = gram_matrix + (members - 1.0) * identity
    projection = jnp.dot(scaled.astype(jnp.float32), innovation, precision=lax.Precision.HIGHEST)
    norm_a = jnp.sqrt(jnp.sum(system * system))
    upper_iter = system / norm_a
    lower_iter = identity
    for sweep in range(NS_ITERS):
        upper_b = upper_iter.astype(jnp.bfloat16)
        lower_b = lower_iter.astype(jnp.bfloat16)
        half_step = (1.5 * identity - 0.5 * product(lower_b, upper_b, ((1,), (0,)))).astype(
            jnp.bfloat16
        )
        if sweep + 1 < NS_ITERS:
            upper_iter = product(upper_b, half_step, ((1,), (0,)))
        lower_iter = product(half_step, lower_b, ((1,), (0,)))
    invroot = lower_iter / jnp.sqrt(norm_a)
    inner_w = jnp.dot(invroot, projection, precision=lax.Precision.HIGHEST)
    mean_w = jnp.dot(invroot, inner_w, precision=lax.Precision.HIGHEST)
    transform = jnp.sqrt(members - 1.0) * invroot + mean_w[:, None]
    return transform.astype(jnp.bfloat16).T


def shift_tiles(block, step):
    count = lax.axis_size("tile")
    return lax.ppermute(block, "tile", [(i, (i + step) % count) for i in range(count)])


def send_order(count):
    return [count - 1, *range(1, count - 1)]


def on_device(hx, obs_value, obs_rinv, obs_index, loc_weight, state):
    rows = hx.shape[0]
    count = lax.axis_size("member")
    position = lax.axis_index("member").astype(jnp.int32).reshape(1)
    steps = send_order(count)

    def send_chunk(chunk):
        return {step: swap(cut(position, state, step, chunk, count), step) for step in steps}

    arrived = [send_chunk(0)]

    pad = jnp.zeros((14, hx.shape[1]), hx.dtype)
    stacked = jnp.concatenate([hx, obs_value[None], obs_rinv[None], pad], axis=0)
    low = shift_tiles(stacked[:, -LOC:], 1)
    high = shift_tiles(stacked[:, :LOC], -1)
    limit = hx.shape[1] - WINDOW + 2 * LOC - LANES
    starts = jnp.minimum(jnp.min(obs_index, axis=1) // LANES * LANES, limit)
    picked, obs_pair = pick(position, starts, obs_index, stacked, low, high, rows)
    others = {step: swap(picked[step], step) for step in steps}
    obs_block = jnp.concatenate([picked[0]] + [others[s] for s in range(1, count)], axis=0)

    for chunk in range(1, CHUNKS):
        arrived.append(send_chunk(chunk))

    transform = analysis(obs_block, obs_pair, loc_weight[0])

    buffer, returned = None, []
    for chunk in range(CHUNKS):
        received = [arrived[chunk][step] for step in range(1, count)]
        buffer, *others = update_state(position, transform, state, received, chunk, buffer)
        returned.append({step: swap(others[step - 1], step) for step in steps})
    for chunk in range(CHUNKS):
        for step in steps:
            buffer = place(position, buffer, returned[chunk][step], step, chunk)
    return buffer


def solution(mesh):
    in_specs = (
        P("member", "tile"),
        P("tile"),
        P("tile"),
        P("tile", None),
        P(("tile", "member"), None),
        P("member", "tile"),
    )
    out_specs = P("member", "tile")
    return jax.shard_map(
        on_device, mesh=mesh, in_specs=in_specs, out_specs=out_specs, check_vma=False
    )
```

```python
import functools

import jax
import jax.numpy as jnp
from jax import lax
from jax.experimental import pallas as pl
from jax.experimental.pallas import tpu as pltpu
from jax.sharding import PartitionSpec as P


LOC = 1024
NS_ITERS = 3
LANES = 128
WINDOW = 2 * LOC
CHUNKS = 2
BLOCK = 512


def partners(count, step):
    return [(i, i ^ step) for i in range(count)]


def swap(block, step):
    return lax.ppermute(block, "member", partners(lax.axis_size("member"), step))


def cut_kernel(first, bands, pos_ref, state_ref, out_ref, held, in_sem, out_sem):
    rows, width = out_ref.shape
    start = pl.multiple_of(first(pos_ref[0]) * width, LANES)
    band = rows // bands
    reads, writes = [], []
    for k in range(bands):
        part = pl.ds(k * band, band)
        reads.append(
            pltpu.make_async_copy(
                state_ref.at[part, pl.ds(start, width)], held.at[part], in_sem.at[k]
            )
        )
        writes.append(pltpu.make_async_copy(held.at[part], out_ref.at[part], out_sem.at[k]))
    for copy in reads:
        copy.start()
    for read, write in zip(reads, writes):
        read.wait()
        write.start()
    for copy in writes:
        copy.wait()


def cut(position, state, step, chunk, count):
    rows, total = state.shape
    width = total // (count * CHUNKS)
    bands = max(rows // 32, 1)
    return pl.pallas_call(
        functools.partial(cut_kernel, lambda pos: (pos ^ step) * CHUNKS + chunk, bands),
        in_specs=[
            pl.BlockSpec(memory_space=pltpu.SMEM),
            pl.BlockSpec(memory_space=pl.ANY),
        ],
        out_specs=pl.BlockSpec(memory_space=pl.ANY),
        scratch_shapes=[
            pltpu.VMEM((rows, width), state.dtype),
            pltpu.SemaphoreType.DMA((bands,)),
            pltpu.SemaphoreType.DMA((bands,)),
        ],
        out_shape=jax.ShapeDtypeStruct((rows, width), state.dtype),
        cost_estimate=pl.CostEstimate(
            flops=0, transcendentals=0, bytes_accessed=2 * rows * width
        ),
    )(position, state)


def pick_kernel(pos_ref, start_ref, index_ref, own_ref, low_ref, high_ref, out_ref, pair_ref, pool):
    step = pl.program_id(0)
    own = own_ref.shape[1]
    span = WINDOW + LANES

    @pl.when(step == 0)
    def _():
        pool[:, :LOC] = low_ref[...]
        pool[:, LOC : LOC + own] = own_ref[...]
        pool[:, LOC + own :] = high_ref[...]

    start = pl.multiple_of(start_ref[pos_ref[0] ^ step], LANES)
    relative = index_ref[0] - start
    window = pool[:, pl.ds(start, span)]
    half = LOC // 4
    for part in range(4):
        where = relative[:, part * half : (part + 1) * half]
        hot = lax.broadcasted_iota(jnp.int32, (span, half), 0) == where
        hot = jnp.where(hot, 1.0, 0.0).astype(jnp.bfloat16)
        picked = jnp.dot(window, hot, preferred_element_type=jnp.float32)
        picked = picked.astype(jnp.bfloat16)
        out_ref[0, :, part * half : (part + 1) * half] = picked[: out_ref.shape[1]]

        @pl.when(step == 0)
        def _():
            pair_ref[:, part * half : (part + 1) * half] = picked[out_ref.shape[1] :]


def pick(position, starts, index, own, low, high, members):
    count = index.shape[0]
    rows, width = own.shape
    whole = lambda shape: pl.BlockSpec(shape, lambda i, pos, start: (0,) * len(shape))
    return pl.pallas_call(
        pick_kernel,
        grid_spec=pltpu.PrefetchScalarGridSpec(
            num_scalar_prefetch=2,
            grid=(count,),
            in_specs=[
                pl.BlockSpec((1, 1, LOC), lambda i, pos, start: (pos[0] ^ i, 0, 0)),
                whole(own.shape),
                whole(low.shape),
                whole(high.shape),
            ],
            out_specs=[
                pl.BlockSpec((1, members, LOC), lambda i, pos, start: (i, 0, 0)),
                whole((rows - members, LOC)),
            ],
            scratch_shapes=[pltpu.VMEM((rows, width + 2 * LOC), jnp.bfloat16)],
        ),
        compiler_params=pltpu.CompilerParams(vmem_limit_bytes=20 << 20),
        out_shape=[
            jax.ShapeDtypeStruct((count, members, LOC), jnp.bfloat16),
            jax.ShapeDtypeStruct((rows - members, LOC), jnp.bfloat16),
        ],
        cost_estimate=pl.CostEstimate(
            flops=2 * count * rows * (WINDOW + LANES) * LOC,
            transcendentals=0,
            bytes_accessed=2 * rows * width + 2 * count * rows * LOC,
        ),
    )(position, starts, index.reshape(count, 1, LOC), own, low, high)


def update_kernel(count, aliased, pos_ref, transform_ref, *refs):
    blocks = refs[:count]
    outs = refs[count + aliased : 2 * count + aliased]
    pert = refs[-1]
    rows = blocks[0].shape[0]
    values = [block[...].astype(jnp.float32) for block in blocks]
    total = jnp.sum(values[0], axis=0, keepdims=True)
    for value in values[1:]:
        total += jnp.sum(value, axis=0, keepdims=True)
    mean = total / (count * rows)
    for k, value in enumerate(values):
        pert[k * rows : (k + 1) * rows, :] = (value - mean).astype(jnp.bfloat16)
    combined = jnp.dot(transform_ref[...], pert[...], preferred_element_type=jnp.float32)
    result = (mean + combined).astype(jnp.bfloat16)
    for k in range(count):
        outs[k][...] = result[k * rows : (k + 1) * rows]


def update_state(position, transform, state, received, chunk, buffer):
    rows, total = state.shape
    count = len(received) + 1
    members = transform.shape[0]
    width = received[0].shape[1]
    block = min(BLOCK, width)
    per = width // block
    own = pl.BlockSpec((rows, block), lambda i, pos: (0, (pos[0] * CHUNKS + chunk) * per + i))
    plain = pl.BlockSpec((rows, block), lambda i, pos: (0, i))
    aliased = 0 if buffer is None else 1
    extra = [] if buffer is None else [pl.BlockSpec(memory_space=pl.ANY)]
    return pl.pallas_call(
        functools.partial(update_kernel, count, aliased),
        grid_spec=pltpu.PrefetchScalarGridSpec(
            num_scalar_prefetch=1,
            grid=(per,),
            in_specs=[pl.BlockSpec((members, members), lambda i, pos: (0, 0)), own]
            + [plain] * (count - 1)
            + extra,
            out_specs=[own] + [plain] * (count - 1),
            scratch_shapes=[pltpu.VMEM((members, block), jnp.bfloat16)],
        ),
        out_shape=[jax.ShapeDtypeStruct((rows, total), state.dtype)]
        + [jax.ShapeDtypeStruct((rows, width), state.dtype)] * (count - 1),
        input_output_aliases={} if buffer is None else {2 + count: 0},
        compiler_params=pltpu.CompilerParams(vmem_limit_bytes=16 << 20),
        cost_estimate=pl.CostEstimate(
            flops=2 * members * members * width,
            transcendentals=0,
            bytes_accessed=4 * members * width + 2 * members * members,
        ),
    )(position, transform, state, *received, *([] if buffer is None else [buffer]))


def place_kernel(first, pos_ref, piece_ref, buffer_ref, out_ref, sem):
    width = piece_ref.shape[1]
    start = pl.multiple_of(first(pos_ref[0]) * width, LANES)
    copy = pltpu.make_async_copy(piece_ref, out_ref.at[:, pl.ds(start, width)], sem)
    copy.start()
    copy.wait()


def place(position, buffer, piece, step, chunk):
    rows, width = piece.shape
    return pl.pallas_call(
        functools.partial(place_kernel, lambda pos: (pos ^ step) * CHUNKS + chunk),
        in_specs=[
            pl.BlockSpec(memory_space=pltpu.SMEM),
            pl.BlockSpec(memory_space=pl.ANY),
            pl.BlockSpec(memory_space=pl.ANY),
        ],
        out_specs=pl.BlockSpec(memory_space=pl.ANY),
        scratch_shapes=[pltpu.SemaphoreType.DMA],
        compiler_params=pltpu.CompilerParams(vmem_limit_bytes=1 << 20),
        out_shape=jax.ShapeDtypeStruct(buffer.shape, buffer.dtype),
        input_output_aliases={2: 0},
        cost_estimate=pl.CostEstimate(
            flops=0, transcendentals=0, bytes_accessed=2 * rows * width
        ),
    )(position, piece, buffer)


def product(left, right, dims):
    return lax.dot_general(left, right, (dims, ((), ())), preferred_element_type=jnp.float32)


def analysis(obs_block, obs_pair, loc_row):
    members = obs_block.shape[0]
    block_f = obs_block.astype(jnp.float32)
    obs_mean = jnp.mean(block_f, axis=0)
    obs_root = jnp.sqrt(obs_pair[1].astype(jnp.float32) * loc_row)
    scaled = ((block_f - obs_mean) * obs_root).astype(jnp.bfloat16)
    innovation = (obs_pair[0].astype(jnp.float32) - obs_mean) * obs_root
    gram_matrix = product(scaled, scaled, ((1,), (1,)))
    identity = jnp.eye(members, dtype=jnp.float32)
    system = gram_matrix + (members - 1.0) * identity
    projection = jnp.dot(scaled.astype(jnp.float32), innovation, precision=lax.Precision.HIGHEST)
    norm_a = jnp.sqrt(jnp.sum(system * system))
    upper_iter = system / norm_a
    lower_iter = identity
    for sweep in range(NS_ITERS):
        upper_b = upper_iter.astype(jnp.bfloat16)
        lower_b = lower_iter.astype(jnp.bfloat16)
        half_step = (1.5 * identity - 0.5 * product(lower_b, upper_b, ((1,), (0,)))).astype(
            jnp.bfloat16
        )
        if sweep + 1 < NS_ITERS:
            upper_iter = product(upper_b, half_step, ((1,), (0,)))
        lower_iter = product(half_step, lower_b, ((1,), (0,)))
    invroot = lower_iter / jnp.sqrt(norm_a)
    inner_w = jnp.dot(invroot, projection, precision=lax.Precision.HIGHEST)
    mean_w = jnp.dot(invroot, inner_w, precision=lax.Precision.HIGHEST)
    transform = jnp.sqrt(members - 1.0) * invroot + mean_w[:, None]
    return transform.astype(jnp.bfloat16).T


def shift_tiles(block, step):
    count = lax.axis_size("tile")
    return lax.ppermute(block, "tile", [(i, (i + step) % count) for i in range(count)])


def send_order(count):
    return [count - 1, *range(1, count - 1)]


def on_device(hx, obs_value, obs_rinv, obs_index, loc_weight, state):
    rows = hx.shape[0]
    count = lax.axis_size("member")
    position = lax.axis_index("member").astype(jnp.int32).reshape(1)
    steps = send_order(count)

    def send_chunk(chunk, order):
        return {step: swap(cut(position, state, step, chunk, count), step) for step in order}

    arrived = [send_chunk(0, steps[:1])]
    arrived[0] |= send_chunk(0, steps[1:])

    pad = jnp.zeros((14, hx.shape[1]), hx.dtype)
    stacked = jnp.concatenate([hx, obs_value[None], obs_rinv[None], pad], axis=0)
    low = shift_tiles(stacked[:, -LOC:], 1)
    high = shift_tiles(stacked[:, :LOC], -1)
    limit = hx.shape[1] - WINDOW + 2 * LOC - LANES
    starts = jnp.minimum(jnp.min(obs_index, axis=1) // LANES * LANES, limit)
    picked, obs_pair = pick(position, starts, obs_index, stacked, low, high, rows)
    others = {step: swap(picked[step], step) for step in steps}
    obs_block = jnp.concatenate([picked[0]] + [others[s] for s in range(1, count)], axis=0)

    for chunk in range(1, CHUNKS):
        arrived.append(send_chunk(chunk, steps))

    transform = analysis(obs_block, obs_pair, loc_weight[0])

    buffer, returned = None, []
    for chunk in range(CHUNKS):
        received = [arrived[chunk][step] for step in range(1, count)]
        buffer, *others = update_state(position, transform, state, received, chunk, buffer)
        returned.append({step: swap(others[step - 1], step) for step in steps})
    for chunk in range(CHUNKS):
        for step in steps:
            buffer = place(position, buffer, returned[chunk][step], step, chunk)
    return buffer


def solution(mesh):
    in_specs = (
        P("member", "tile"),
        P("tile"),
        P("tile"),
        P("tile", None),
        P(("tile", "member"), None),
        P("member", "tile"),
    )
    out_specs = P("member", "tile")
    return jax.shard_map(
        on_device, mesh=mesh, in_specs=in_specs, out_specs=out_specs, check_vma=False
    )
```

```python
import functools

import jax
import jax.numpy as jnp
from jax import lax
from jax.experimental import pallas as pl
from jax.experimental.pallas import tpu as pltpu
from jax.sharding import PartitionSpec as P


LOC = 1024
NS_ITERS = 3
LANES = 128
WINDOW = 2 * LOC
CHUNKS = 2
BLOCK = 512


def partners(count, step):
    return [(i, i ^ step) for i in range(count)]


def swap(block, step):
    return lax.ppermute(block, "member", partners(lax.axis_size("member"), step))


def cut(position, state, step, chunk, count):
    rows, total = state.shape
    width = total // (count * CHUNKS)
    start = ((position[0] ^ step) * CHUNKS + chunk) * width
    return lax.dynamic_slice(state, (0, start), (rows, width))


def pick_kernel(pos_ref, start_ref, index_ref, own_ref, low_ref, high_ref, out_ref, pair_ref, pool):
    step = pl.program_id(0)
    own = own_ref.shape[1]
    span = WINDOW + LANES

    @pl.when(step == 0)
    def _():
        pool[:, :LOC] = low_ref[...]
        pool[:, LOC : LOC + own] = own_ref[...]
        pool[:, LOC + own :] = high_ref[...]

    start = pl.multiple_of(start_ref[pos_ref[0] ^ step], LANES)
    relative = index_ref[0] - start
    window = pool[:, pl.ds(start, span)]
    half = LOC // 4
    for part in range(4):
        where = relative[:, part * half : (part + 1) * half]
        hot = lax.broadcasted_iota(jnp.int32, (span, half), 0) == where
        hot = jnp.where(hot, 1.0, 0.0).astype(jnp.bfloat16)
        picked = jnp.dot(window, hot, preferred_element_type=jnp.float32)
        picked = picked.astype(jnp.bfloat16)
        out_ref[0, :, part * half : (part + 1) * half] = picked[: out_ref.shape[1]]

        @pl.when(step == 0)
        def _():
            pair_ref[:, part * half : (part + 1) * half] = picked[out_ref.shape[1] :]


def pick(position, starts, index, own, low, high, members):
    count = index.shape[0]
    rows, width = own.shape
    whole = lambda shape: pl.BlockSpec(shape, lambda i, pos, start: (0,) * len(shape))
    return pl.pallas_call(
        pick_kernel,
        grid_spec=pltpu.PrefetchScalarGridSpec(
            num_scalar_prefetch=2,
            grid=(count,),
            in_specs=[
                pl.BlockSpec((1, 1, LOC), lambda i, pos, start: (pos[0] ^ i, 0, 0)),
                whole(own.shape),
                whole(low.shape),
                whole(high.shape),
            ],
            out_specs=[
                pl.BlockSpec((1, members, LOC), lambda i, pos, start: (i, 0, 0)),
                whole((rows - members, LOC)),
            ],
            scratch_shapes=[pltpu.VMEM((rows, width + 2 * LOC), jnp.bfloat16)],
        ),
        compiler_params=pltpu.CompilerParams(vmem_limit_bytes=20 << 20),
        out_shape=[
            jax.ShapeDtypeStruct((count, members, LOC), jnp.bfloat16),
            jax.ShapeDtypeStruct((rows - members, LOC), jnp.bfloat16),
        ],
        cost_estimate=pl.CostEstimate(
            flops=2 * count * rows * (WINDOW + LANES) * LOC,
            transcendentals=0,
            bytes_accessed=2 * rows * width + 2 * count * rows * LOC,
        ),
    )(position, starts, index.reshape(count, 1, LOC), own, low, high)


def update_kernel(count, aliased, pos_ref, transform_ref, *refs):
    blocks = refs[:count]
    outs = refs[count + aliased : 2 * count + aliased]
    pert = refs[-1]
    rows = blocks[0].shape[0]
    values = [block[...].astype(jnp.float32) for block in blocks]
    total = jnp.sum(values[0], axis=0, keepdims=True)
    for value in values[1:]:
        total += jnp.sum(value, axis=0, keepdims=True)
    mean = total / (count * rows)
    for k, value in enumerate(values):
        pert[k * rows : (k + 1) * rows, :] = (value - mean).astype(jnp.bfloat16)
    combined = jnp.dot(transform_ref[...], pert[...], preferred_element_type=jnp.float32)
    result = (mean + combined).astype(jnp.bfloat16)
    for k in range(count):
        outs[k][...] = result[k * rows : (k + 1) * rows]


def update_state(position, transform, state, received, chunk, buffer):
    rows, total = state.shape
    count = len(received) + 1
    members = transform.shape[0]
    width = received[0].shape[1]
    block = min(BLOCK, width)
    per = width // block
    own = pl.BlockSpec((rows, block), lambda i, pos: (0, (pos[0] * CHUNKS + chunk) * per + i))
    plain = pl.BlockSpec((rows, block), lambda i, pos: (0, i))
    aliased = 0 if buffer is None else 1
    extra = [] if buffer is None else [pl.BlockSpec(memory_space=pl.ANY)]
    return pl.pallas_call(
        functools.partial(update_kernel, count, aliased),
        grid_spec=pltpu.PrefetchScalarGridSpec(
            num_scalar_prefetch=1,
            grid=(per,),
            in_specs=[pl.BlockSpec((members, members), lambda i, pos: (0, 0)), own]
            + [plain] * (count - 1)
            + extra,
            out_specs=[own] + [plain] * (count - 1),
            scratch_shapes=[pltpu.VMEM((members, block), jnp.bfloat16)],
        ),
        out_shape=[jax.ShapeDtypeStruct((rows, total), state.dtype)]
        + [jax.ShapeDtypeStruct((rows, width), state.dtype)] * (count - 1),
        input_output_aliases={} if buffer is None else {2 + count: 0},
        compiler_params=pltpu.CompilerParams(vmem_limit_bytes=16 << 20),
        cost_estimate=pl.CostEstimate(
            flops=2 * members * members * width,
            transcendentals=0,
            bytes_accessed=4 * members * width + 2 * members * members,
        ),
    )(position, transform, state, *received, *([] if buffer is None else [buffer]))


def place_kernel(first, pos_ref, piece_ref, buffer_ref, out_ref, sem):
    width = piece_ref.shape[1]
    start = pl.multiple_of(first(pos_ref[0]) * width, LANES)
    copy = pltpu.make_async_copy(piece_ref, out_ref.at[:, pl.ds(start, width)], sem)
    copy.start()
    copy.wait()


def place(position, buffer, piece, step, chunk):
    rows, width = piece.shape
    return pl.pallas_call(
        functools.partial(place_kernel, lambda pos: (pos ^ step) * CHUNKS + chunk),
        in_specs=[
            pl.BlockSpec(memory_space=pltpu.SMEM),
            pl.BlockSpec(memory_space=pl.ANY),
            pl.BlockSpec(memory_space=pl.ANY),
        ],
        out_specs=pl.BlockSpec(memory_space=pl.ANY),
        scratch_shapes=[pltpu.SemaphoreType.DMA],
        compiler_params=pltpu.CompilerParams(vmem_limit_bytes=1 << 20),
        out_shape=jax.ShapeDtypeStruct(buffer.shape, buffer.dtype),
        input_output_aliases={2: 0},
        cost_estimate=pl.CostEstimate(
            flops=0, transcendentals=0, bytes_accessed=2 * rows * width
        ),
    )(position, piece, buffer)


def product(left, right, dims):
    return lax.dot_general(left, right, (dims, ((), ())), preferred_element_type=jnp.float32)


def analysis(obs_block, obs_pair, loc_row):
    members = obs_block.shape[0]
    block_f = obs_block.astype(jnp.float32)
    obs_mean = jnp.mean(block_f, axis=0)
    obs_root = jnp.sqrt(obs_pair[1].astype(jnp.float32) * loc_row)
    scaled = ((block_f - obs_mean) * obs_root).astype(jnp.bfloat16)
    innovation = (obs_pair[0].astype(jnp.float32) - obs_mean) * obs_root
    gram_matrix = product(scaled, scaled, ((1,), (1,)))
    identity = jnp.eye(members, dtype=jnp.float32)
    system = gram_matrix + (members - 1.0) * identity
    projection = jnp.dot(scaled.astype(jnp.float32), innovation, precision=lax.Precision.HIGHEST)
    norm_a = jnp.sqrt(jnp.sum(system * system))
    upper_iter = system / norm_a
    lower_iter = identity
    for sweep in range(NS_ITERS):
        upper_b = upper_iter.astype(jnp.bfloat16)
        lower_b = lower_iter.astype(jnp.bfloat16)
        half_step = (1.5 * identity - 0.5 * product(lower_b, upper_b, ((1,), (0,)))).astype(
            jnp.bfloat16
        )
        if sweep + 1 < NS_ITERS:
            upper_iter = product(upper_b, half_step, ((1,), (0,)))
        lower_iter = product(half_step, lower_b, ((1,), (0,)))
    invroot = lower_iter / jnp.sqrt(norm_a)
    inner_w = jnp.dot(invroot, projection, precision=lax.Precision.HIGHEST)
    mean_w = jnp.dot(invroot, inner_w, precision=lax.Precision.HIGHEST)
    transform = jnp.sqrt(members - 1.0) * invroot + mean_w[:, None]
    return transform.astype(jnp.bfloat16).T


def shift_tiles(block, step):
    count = lax.axis_size("tile")
    return lax.ppermute(block, "tile", [(i, (i + step) % count) for i in range(count)])


def send_order(count):
    return [count - 1, *range(1, count - 1)]


def on_device(hx, obs_value, obs_rinv, obs_index, loc_weight, state):
    rows = hx.shape[0]
    count = lax.axis_size("member")
    position = lax.axis_index("member").astype(jnp.int32).reshape(1)
    steps = send_order(count)

    source = state

    def send_chunk(chunk, order):
        nonlocal source
        sent = {}
        for step in order:
            piece = cut(position, source, step, chunk, count)
            source, piece = lax.optimization_barrier((source, piece))
            sent[step] = swap(piece, step)
        return sent

    arrived = [send_chunk(0, steps[:1])]
    arrived[0] |= send_chunk(0, steps[1:])

    pad = jnp.zeros((14, hx.shape[1]), hx.dtype)
    stacked = jnp.concatenate([hx, obs_value[None], obs_rinv[None], pad], axis=0)
    low = shift_tiles(stacked[:, -LOC:], 1)
    high = shift_tiles(stacked[:, :LOC], -1)
    limit = hx.shape[1] - WINDOW + 2 * LOC - LANES
    starts = jnp.minimum(jnp.min(obs_index, axis=1) // LANES * LANES, limit)
    picked, obs_pair = pick(position, starts, obs_index, stacked, low, high, rows)
    others = {step: swap(picked[step], step) for step in steps}
    obs_block = jnp.concatenate([picked[0]] + [others[s] for s in range(1, count)], axis=0)

    for chunk in range(1, CHUNKS):
        arrived.append(send_chunk(chunk, steps))

    transform = analysis(obs_block, obs_pair, loc_weight[0])

    buffer, returned = None, []
    back = steps[:0:-1] + steps[:1]
    for chunk in range(CHUNKS):
        received = [arrived[chunk][step] for step in range(1, count)]
        buffer, *others = update_state(position, transform, state, received, chunk, buffer)
        returned.append({step: swap(others[step - 1], step) for step in back[:-1]})
        returned[-1][back[-1]] = swap(others[back[-1] - 1], back[-1])
    for chunk in range(CHUNKS):
        for step in back:
            buffer = place(position, buffer, returned[chunk][step], step, chunk)
    return buffer


def solution(mesh):
    in_specs = (
        P("member", "tile"),
        P("tile"),
        P("tile"),
        P("tile", None),
        P(("tile", "member"), None),
        P("member", "tile"),
    )
    out_specs = P("member", "tile")
    return jax.shard_map(
        on_device, mesh=mesh, in_specs=in_specs, out_specs=out_specs, check_vma=False
    )
```

```python
import functools

import jax
import jax.numpy as jnp
from jax import lax
from jax.experimental import pallas as pl
from jax.experimental.pallas import tpu as pltpu
from jax.sharding import PartitionSpec as P


LOC = 1024
NS_ITERS = 3
LANES = 128
WINDOW = 2 * LOC
CHUNKS = 2
BLOCK = 512


def partners(count, step):
    return [(i, i ^ step) for i in range(count)]


def swap(block, step):
    return lax.ppermute(block, "member", partners(lax.axis_size("member"), step))


def cut(position, state, step, chunk, count, part=(0, 1)):
    rows, total = state.shape
    width = total // (count * CHUNKS)
    low, high = int(part[0] * width), int(part[1] * width)
    start = ((position[0] ^ step) * CHUNKS + chunk) * width + low
    return lax.dynamic_slice(state, (0, start), (rows, high - low))


def pick_kernel(pos_ref, start_ref, index_ref, own_ref, low_ref, high_ref, out_ref, pair_ref, pool):
    step = pl.program_id(0)
    own = own_ref.shape[1]
    span = WINDOW + LANES

    @pl.when(step == 0)
    def _():
        pool[:, :LOC] = low_ref[...]
        pool[:, LOC : LOC + own] = own_ref[...]
        pool[:, LOC + own :] = high_ref[...]

    start = pl.multiple_of(start_ref[pos_ref[0] ^ step], LANES)
    relative = index_ref[0] - start
    window = pool[:, pl.ds(start, span)]
    half = LOC // 4
    for part in range(4):
        where = relative[:, part * half : (part + 1) * half]
        hot = lax.broadcasted_iota(jnp.int32, (span, half), 0) == where
        hot = jnp.where(hot, 1.0, 0.0).astype(jnp.bfloat16)
        picked = jnp.dot(window, hot, preferred_element_type=jnp.float32)
        picked = picked.astype(jnp.bfloat16)
        out_ref[0, :, part * half : (part + 1) * half] = picked[: out_ref.shape[1]]

        @pl.when(step == 0)
        def _():
            pair_ref[:, part * half : (part + 1) * half] = picked[out_ref.shape[1] :]


def pick(position, starts, index, own, low, high, members):
    count = index.shape[0]
    rows, width = own.shape
    whole = lambda shape: pl.BlockSpec(shape, lambda i, pos, start: (0,) * len(shape))
    return pl.pallas_call(
        pick_kernel,
        grid_spec=pltpu.PrefetchScalarGridSpec(
            num_scalar_prefetch=2,
            grid=(count,),
            in_specs=[
                pl.BlockSpec((1, 1, LOC), lambda i, pos, start: (pos[0] ^ i, 0, 0)),
                whole(own.shape),
                whole(low.shape),
                whole(high.shape),
            ],
            out_specs=[
                pl.BlockSpec((1, members, LOC), lambda i, pos, start: (i, 0, 0)),
                whole((rows - members, LOC)),
            ],
            scratch_shapes=[pltpu.VMEM((rows, width + 2 * LOC), jnp.bfloat16)],
        ),
        compiler_params=pltpu.CompilerParams(vmem_limit_bytes=20 << 20),
        out_shape=[
            jax.ShapeDtypeStruct((count, members, LOC), jnp.bfloat16),
            jax.ShapeDtypeStruct((rows - members, LOC), jnp.bfloat16),
        ],
        cost_estimate=pl.CostEstimate(
            flops=2 * count * rows * (WINDOW + LANES) * LOC,
            transcendentals=0,
            bytes_accessed=2 * rows * width + 2 * count * rows * LOC,
        ),
    )(position, starts, index.reshape(count, 1, LOC), own, low, high)


def update_kernel(count, aliased, pos_ref, transform_ref, *refs):
    blocks = refs[:count]
    outs = refs[count + aliased : 2 * count + aliased]
    pert = refs[-1]
    rows = blocks[0].shape[0]
    values = [block[...].astype(jnp.float32) for block in blocks]
    total = jnp.sum(values[0], axis=0, keepdims=True)
    for value in values[1:]:
        total += jnp.sum(value, axis=0, keepdims=True)
    mean = total / (count * rows)
    for k, value in enumerate(values):
        pert[k * rows : (k + 1) * rows, :] = (value - mean).astype(jnp.bfloat16)
    combined = jnp.dot(transform_ref[...], pert[...], preferred_element_type=jnp.float32)
    result = (mean + combined).astype(jnp.bfloat16)
    for k in range(count):
        outs[k][...] = result[k * rows : (k + 1) * rows]


def update_state(position, transform, state, received, chunk, buffer):
    rows, total = state.shape
    count = len(received) + 1
    members = transform.shape[0]
    width = received[0].shape[1]
    block = min(BLOCK, width)
    per = width // block
    own = pl.BlockSpec((rows, block), lambda i, pos: (0, (pos[0] * CHUNKS + chunk) * per + i))
    plain = pl.BlockSpec((rows, block), lambda i, pos: (0, i))
    aliased = 0 if buffer is None else 1
    extra = [] if buffer is None else [pl.BlockSpec(memory_space=pl.ANY)]
    return pl.pallas_call(
        functools.partial(update_kernel, count, aliased),
        grid_spec=pltpu.PrefetchScalarGridSpec(
            num_scalar_prefetch=1,
            grid=(per,),
            in_specs=[pl.BlockSpec((members, members), lambda i, pos: (0, 0)), own]
            + [plain] * (count - 1)
            + extra,
            out_specs=[own] + [plain] * (count - 1),
            scratch_shapes=[pltpu.VMEM((members, block), jnp.bfloat16)],
        ),
        out_shape=[jax.ShapeDtypeStruct((rows, total), state.dtype)]
        + [jax.ShapeDtypeStruct((rows, width), state.dtype)] * (count - 1),
        input_output_aliases={} if buffer is None else {2 + count: 0},
        compiler_params=pltpu.CompilerParams(vmem_limit_bytes=16 << 20),
        cost_estimate=pl.CostEstimate(
            flops=2 * members * members * width,
            transcendentals=0,
            bytes_accessed=4 * members * width + 2 * members * members,
        ),
    )(position, transform, state, *received, *([] if buffer is None else [buffer]))


def place_kernel(first, pos_ref, piece_ref, buffer_ref, out_ref, sem):
    width = piece_ref.shape[1]
    start = pl.multiple_of(first(pos_ref[0]) * width, LANES)
    copy = pltpu.make_async_copy(piece_ref, out_ref.at[:, pl.ds(start, width)], sem)
    copy.start()
    copy.wait()


def place(position, buffer, piece, step, chunk):
    rows, width = piece.shape
    return pl.pallas_call(
        functools.partial(place_kernel, lambda pos: (pos ^ step) * CHUNKS + chunk),
        in_specs=[
            pl.BlockSpec(memory_space=pltpu.SMEM),
            pl.BlockSpec(memory_space=pl.ANY),
            pl.BlockSpec(memory_space=pl.ANY),
        ],
        out_specs=pl.BlockSpec(memory_space=pl.ANY),
        scratch_shapes=[pltpu.SemaphoreType.DMA],
        compiler_params=pltpu.CompilerParams(vmem_limit_bytes=1 << 20),
        out_shape=jax.ShapeDtypeStruct(buffer.shape, buffer.dtype),
        input_output_aliases={2: 0},
        cost_estimate=pl.CostEstimate(
            flops=0, transcendentals=0, bytes_accessed=2 * rows * width
        ),
    )(position, piece, buffer)


def product(left, right, dims):
    return lax.dot_general(left, right, (dims, ((), ())), preferred_element_type=jnp.float32)


def analysis(obs_block, obs_pair, loc_row):
    members = obs_block.shape[0]
    block_f = obs_block.astype(jnp.float32)
    obs_mean = jnp.mean(block_f, axis=0)
    obs_root = jnp.sqrt(obs_pair[1].astype(jnp.float32) * loc_row)
    scaled = ((block_f - obs_mean) * obs_root).astype(jnp.bfloat16)
    innovation = (obs_pair[0].astype(jnp.float32) - obs_mean) * obs_root
    gram_matrix = product(scaled, scaled, ((1,), (1,)))
    identity = jnp.eye(members, dtype=jnp.float32)
    system = gram_matrix + (members - 1.0) * identity
    projection = jnp.dot(scaled.astype(jnp.float32), innovation, precision=lax.Precision.HIGHEST)
    norm_a = jnp.sqrt(jnp.sum(system * system))
    upper_iter = system / norm_a
    lower_iter = identity
    for sweep in range(NS_ITERS):
        upper_b = upper_iter.astype(jnp.bfloat16)
        lower_b = lower_iter.astype(jnp.bfloat16)
        half_step = (1.5 * identity - 0.5 * product(lower_b, upper_b, ((1,), (0,)))).astype(
            jnp.bfloat16
        )
        if sweep + 1 < NS_ITERS:
            upper_iter = product(upper_b, half_step, ((1,), (0,)))
        lower_iter = product(half_step, lower_b, ((1,), (0,)))
    invroot = lower_iter / jnp.sqrt(norm_a)
    inner_w = jnp.dot(invroot, projection, precision=lax.Precision.HIGHEST)
    mean_w = jnp.dot(invroot, inner_w, precision=lax.Precision.HIGHEST)
    transform = jnp.sqrt(members - 1.0) * invroot + mean_w[:, None]
    return transform.astype(jnp.bfloat16).T


def shift_tiles(block, step):
    count = lax.axis_size("tile")
    return lax.ppermute(block, "tile", [(i, (i + step) % count) for i in range(count)])


def send_order(count):
    return [count - 1, *range(1, count - 1)]


def on_device(hx, obs_value, obs_rinv, obs_index, loc_weight, state):
    rows = hx.shape[0]
    count = lax.axis_size("member")
    position = lax.axis_index("member").astype(jnp.int32).reshape(1)
    steps = send_order(count)

    source = state

    def send(chunk, step, part=(0, 1)):
        nonlocal source
        piece = cut(position, source, step, chunk, count, part)
        source, piece = lax.optimization_barrier((source, piece))
        return swap(piece, step)

    def send_chunk(chunk, order):
        return {step: send(chunk, step) for step in order}

    head = send(0, steps[0], (0, 0.25))
    rest = send(0, steps[0], (0.25, 1))
    arrived = [send_chunk(0, steps[1:])]
    arrived[0][steps[0]] = jnp.concatenate([head, rest], axis=1)

    pad = jnp.zeros((14, hx.shape[1]), hx.dtype)
    stacked = jnp.concatenate([hx, obs_value[None], obs_rinv[None], pad], axis=0)
    low = shift_tiles(stacked[:, -LOC:], 1)
    high = shift_tiles(stacked[:, :LOC], -1)
    limit = hx.shape[1] - WINDOW + 2 * LOC - LANES
    starts = jnp.minimum(jnp.min(obs_index, axis=1) // LANES * LANES, limit)
    picked, obs_pair = pick(position, starts, obs_index, stacked, low, high, rows)
    others = {step: swap(picked[step], step) for step in steps}
    obs_block = jnp.concatenate([picked[0]] + [others[s] for s in range(1, count)], axis=0)

    for chunk in range(1, CHUNKS):
        arrived.append(send_chunk(chunk, steps))

    transform = analysis(obs_block, obs_pair, loc_weight[0])

    buffer, returned = None, []
    back = steps[:0:-1] + steps[:1]
    for chunk in range(CHUNKS):
        received = [arrived[chunk][step] for step in range(1, count)]
        buffer, *others = update_state(position, transform, state, received, chunk, buffer)
        returned.append({step: swap(others[step - 1], step) for step in back[:-1]})
        returned[-1][back[-1]] = swap(others[back[-1] - 1], back[-1])
    for chunk in range(CHUNKS):
        for step in back:
            buffer = place(position, buffer, returned[chunk][step], step, chunk)
    return buffer


def solution(mesh):
    in_specs = (
        P("member", "tile"),
        P("tile"),
        P("tile"),
        P("tile", None),
        P(("tile", "member"), None),
        P("member", "tile"),
    )
    out_specs = P("member", "tile")
    return jax.shard_map(
        on_device, mesh=mesh, in_specs=in_specs, out_specs=out_specs, check_vma=False
    )
```

```python
import functools

import jax
import jax.numpy as jnp
from jax import lax
from jax.experimental import pallas as pl
from jax.experimental.pallas import tpu as pltpu
from jax.sharding import PartitionSpec as P


LOC = 1024
NS_ITERS = 3
LANES = 128
WINDOW = 2 * LOC
CHUNKS = 2
BLOCK = 512


def partners(count, step):
    return [(i, i ^ step) for i in range(count)]


def swap(block, step):
    return lax.ppermute(block, "member", partners(lax.axis_size("member"), step))


def cut(position, state, step, chunk, count, part=(0, 1)):
    rows, total = state.shape
    width = total // (count * CHUNKS)
    low, high = int(part[0] * width), int(part[1] * width)
    start = ((position[0] ^ step) * CHUNKS + chunk) * width + low
    return lax.dynamic_slice(state, (0, start), (rows, high - low))


def lead_kernel(first, pos_ref, state_ref, out_ref, sem):
    start = pl.multiple_of(first(pos_ref[0]), LANES)
    copy = pltpu.make_async_copy(state_ref.at[:, pl.ds(start, out_ref.shape[1])], out_ref, sem)
    copy.start()
    copy.wait()


def lead_piece(position, state, step, width):
    rows, total = state.shape
    patch = total // lax.axis_size("member")
    return pl.pallas_call(
        functools.partial(lead_kernel, lambda pos: (pos ^ step) * patch),
        in_specs=[
            pl.BlockSpec(memory_space=pltpu.SMEM),
            pl.BlockSpec(memory_space=pl.ANY),
        ],
        out_specs=pl.BlockSpec(memory_space=pltpu.VMEM),
        scratch_shapes=[pltpu.SemaphoreType.DMA],
        out_shape=pltpu.VMEM((rows, width), state.dtype),
        cost_estimate=pl.CostEstimate(
            flops=0, transcendentals=0, bytes_accessed=2 * rows * width
        ),
    )(position, state)


def pick_kernel(pos_ref, start_ref, index_ref, own_ref, low_ref, high_ref, out_ref, pair_ref, pool):
    step = pl.program_id(0)
    own = own_ref.shape[1]
    span = WINDOW + LANES

    @pl.when(step == 0)
    def _():
        pool[:, :LOC] = low_ref[...]
        pool[:, LOC : LOC + own] = own_ref[...]
        pool[:, LOC + own :] = high_ref[...]

    start = pl.multiple_of(start_ref[pos_ref[0] ^ step], LANES)
    relative = index_ref[0] - start
    window = pool[:, pl.ds(start, span)]
    half = LOC // 4
    for part in range(4):
        where = relative[:, part * half : (part + 1) * half]
        hot = lax.broadcasted_iota(jnp.int32, (span, half), 0) == where
        hot = jnp.where(hot, 1.0, 0.0).astype(jnp.bfloat16)
        picked = jnp.dot(window, hot, preferred_element_type=jnp.float32)
        picked = picked.astype(jnp.bfloat16)
        out_ref[0, :, part * half : (part + 1) * half] = picked[: out_ref.shape[1]]

        @pl.when(step == 0)
        def _():
            pair_ref[:, part * half : (part + 1) * half] = picked[out_ref.shape[1] :]


def pick(position, starts, index, own, low, high, members):
    count = index.shape[0]
    rows, width = own.shape
    whole = lambda shape: pl.BlockSpec(shape, lambda i, pos, start: (0,) * len(shape))
    return pl.pallas_call(
        pick_kernel,
        grid_spec=pltpu.PrefetchScalarGridSpec(
            num_scalar_prefetch=2,
            grid=(count,),
            in_specs=[
                pl.BlockSpec((1, 1, LOC), lambda i, pos, start: (pos[0] ^ i, 0, 0)),
                whole(own.shape),
                whole(low.shape),
                whole(high.shape),
            ],
            out_specs=[
                pl.BlockSpec((1, members, LOC), lambda i, pos, start: (i, 0, 0)),
                whole((rows - members, LOC)),
            ],
            scratch_shapes=[pltpu.VMEM((rows, width + 2 * LOC), jnp.bfloat16)],
        ),
        compiler_params=pltpu.CompilerParams(vmem_limit_bytes=20 << 20),
        out_shape=[
            jax.ShapeDtypeStruct((count, members, LOC), jnp.bfloat16),
            jax.ShapeDtypeStruct((rows - members, LOC), jnp.bfloat16),
        ],
        cost_estimate=pl.CostEstimate(
            flops=2 * count * rows * (WINDOW + LANES) * LOC,
            transcendentals=0,
            bytes_accessed=2 * rows * width + 2 * count * rows * LOC,
        ),
    )(position, starts, index.reshape(count, 1, LOC), own, low, high)


def update_kernel(count, aliased, pos_ref, transform_ref, *refs):
    blocks = refs[:count]
    outs = refs[count + aliased : 2 * count + aliased]
    pert = refs[-1]
    rows = blocks[0].shape[0]
    values = [block[...].astype(jnp.float32) for block in blocks]
    total = jnp.sum(values[0], axis=0, keepdims=True)
    for value in values[1:]:
        total += jnp.sum(value, axis=0, keepdims=True)
    mean = total / (count * rows)
    for k, value in enumerate(values):
        pert[k * rows : (k + 1) * rows, :] = (value - mean).astype(jnp.bfloat16)
    combined = jnp.dot(transform_ref[...], pert[...], preferred_element_type=jnp.float32)
    result = (mean + combined).astype(jnp.bfloat16)
    for k in range(count):
        outs[k][...] = result[k * rows : (k + 1) * rows]


def update_state(position, transform, state, received, chunk, buffer):
    rows, total = state.shape
    count = len(received) + 1
    members = transform.shape[0]
    width = received[0].shape[1]
    block = min(BLOCK, width)
    per = width // block
    own = pl.BlockSpec((rows, block), lambda i, pos: (0, (pos[0] * CHUNKS + chunk) * per + i))
    plain = pl.BlockSpec((rows, block), lambda i, pos: (0, i))
    aliased = 0 if buffer is None else 1
    extra = [] if buffer is None else [pl.BlockSpec(memory_space=pl.ANY)]
    return pl.pallas_call(
        functools.partial(update_kernel, count, aliased),
        grid_spec=pltpu.PrefetchScalarGridSpec(
            num_scalar_prefetch=1,
            grid=(per,),
            in_specs=[pl.BlockSpec((members, members), lambda i, pos: (0, 0)), own]
            + [plain] * (count - 1)
            + extra,
            out_specs=[own] + [plain] * (count - 1),
            scratch_shapes=[pltpu.VMEM((members, block), jnp.bfloat16)],
        ),
        out_shape=[jax.ShapeDtypeStruct((rows, total), state.dtype)]
        + [jax.ShapeDtypeStruct((rows, width), state.dtype)] * (count - 1),
        input_output_aliases={} if buffer is None else {2 + count: 0},
        compiler_params=pltpu.CompilerParams(vmem_limit_bytes=16 << 20),
        cost_estimate=pl.CostEstimate(
            flops=2 * members * members * width,
            transcendentals=0,
            bytes_accessed=4 * members * width + 2 * members * members,
        ),
    )(position, transform, state, *received, *([] if buffer is None else [buffer]))


def place_kernel(first, pos_ref, piece_ref, buffer_ref, out_ref, sem):
    width = piece_ref.shape[1]
    start = pl.multiple_of(first(pos_ref[0]), LANES)
    copy = pltpu.make_async_copy(piece_ref, out_ref.at[:, pl.ds(start, width)], sem)
    copy.start()
    copy.wait()


def place(position, buffer, piece, step, offset):
    rows, width = piece.shape
    patch = buffer.shape[1] // lax.axis_size("member")
    return pl.pallas_call(
        functools.partial(place_kernel, lambda pos: (pos ^ step) * patch + offset),
        in_specs=[
            pl.BlockSpec(memory_space=pltpu.SMEM),
            pl.BlockSpec(memory_space=pl.ANY),
            pl.BlockSpec(memory_space=pl.ANY),
        ],
        out_specs=pl.BlockSpec(memory_space=pl.ANY),
        scratch_shapes=[pltpu.SemaphoreType.DMA],
        compiler_params=pltpu.CompilerParams(vmem_limit_bytes=1 << 20),
        out_shape=jax.ShapeDtypeStruct(buffer.shape, buffer.dtype),
        input_output_aliases={2: 0},
        cost_estimate=pl.CostEstimate(
            flops=0, transcendentals=0, bytes_accessed=2 * rows * width
        ),
    )(position, piece, buffer)


def product(left, right, dims):
    return lax.dot_general(left, right, (dims, ((), ())), preferred_element_type=jnp.float32)


def analysis(obs_block, obs_pair, loc_row):
    members = obs_block.shape[0]
    block_f = obs_block.astype(jnp.float32)
    obs_mean = jnp.mean(block_f, axis=0)
    obs_root = jnp.sqrt(obs_pair[1].astype(jnp.float32) * loc_row)
    scaled = ((block_f - obs_mean) * obs_root).astype(jnp.bfloat16)
    innovation = (obs_pair[0].astype(jnp.float32) - obs_mean) * obs_root
    gram_matrix = product(scaled, scaled, ((1,), (1,)))
    identity = jnp.eye(members, dtype=jnp.float32)
    system = gram_matrix + (members - 1.0) * identity
    projection = jnp.dot(scaled.astype(jnp.float32), innovation, precision=lax.Precision.HIGHEST)
    norm_a = jnp.sqrt(jnp.sum(system * system))
    upper_iter = system / norm_a
    lower_iter = identity
    for sweep in range(NS_ITERS):
        upper_b = upper_iter.astype(jnp.bfloat16)
        lower_b = lower_iter.astype(jnp.bfloat16)
        half_step = (1.5 * identity - 0.5 * product(lower_b, upper_b, ((1,), (0,)))).astype(
            jnp.bfloat16
        )
        if sweep + 1 < NS_ITERS:
            upper_iter = product(upper_b, half_step, ((1,), (0,)))
        lower_iter = product(half_step, lower_b, ((1,), (0,)))
    invroot = lower_iter / jnp.sqrt(norm_a)
    inner_w = jnp.dot(invroot, projection, precision=lax.Precision.HIGHEST)
    mean_w = jnp.dot(invroot, inner_w, precision=lax.Precision.HIGHEST)
    transform = jnp.sqrt(members - 1.0) * invroot + mean_w[:, None]
    return transform.astype(jnp.bfloat16).T


def shift_tiles(block, step):
    count = lax.axis_size("tile")
    return lax.ppermute(block, "tile", [(i, (i + step) % count) for i in range(count)])


def send_order(count):
    return [count - 1, *range(1, count - 1)]


def on_device(hx, obs_value, obs_rinv, obs_index, loc_weight, state):
    rows = hx.shape[0]
    count = lax.axis_size("member")
    position = lax.axis_index("member").astype(jnp.int32).reshape(1)
    steps = send_order(count)

    source = state

    def send(chunk, step, part=(0, 1)):
        nonlocal source
        piece = cut(position, source, step, chunk, count, part)
        source, piece = lax.optimization_barrier((source, piece))
        return swap(piece, step)

    def send_chunk(chunk, order):
        return {step: send(chunk, step) for step in order}

    piece = lead_piece(position, source, steps[0], state.shape[1] // (4 * count * CHUNKS))
    source, piece = lax.optimization_barrier((source, piece))
    head = swap(piece, steps[0])
    rest = send(0, steps[0], (0.25, 1))
    arrived = [send_chunk(0, steps[1:])]
    arrived[0][steps[0]] = jnp.concatenate([head, rest], axis=1)

    pad = jnp.zeros((14, hx.shape[1]), hx.dtype)
    stacked = jnp.concatenate([hx, obs_value[None], obs_rinv[None], pad], axis=0)
    low = shift_tiles(stacked[:, -LOC:], 1)
    high = shift_tiles(stacked[:, :LOC], -1)
    limit = hx.shape[1] - WINDOW + 2 * LOC - LANES
    starts = jnp.minimum(jnp.min(obs_index, axis=1) // LANES * LANES, limit)
    picked, obs_pair = pick(position, starts, obs_index, stacked, low, high, rows)
    others = {step: swap(picked[step], step) for step in steps}
    obs_block = jnp.concatenate([picked[0]] + [others[s] for s in range(1, count)], axis=0)

    for chunk in range(1, CHUNKS):
        arrived.append(send_chunk(chunk, steps))

    transform = analysis(obs_block, obs_pair, loc_weight[0])

    buffer, returned = None, []
    back = steps[:0:-1] + steps[:1]
    width = state.shape[1] // (count * CHUNKS)
    for chunk in range(CHUNKS):
        received = [arrived[chunk][step] for step in range(1, count)]
        buffer, *others = update_state(position, transform, state, received, chunk, buffer)
        last = chunk == CHUNKS - 1
        for step in back[:-1]:
            returned.append((swap(others[step - 1], step), step, chunk * width))
        step, cuts = back[-1], [0, width]
        if last:
            cuts = [0, width * 3 // 4, width]
        for low, high in zip(cuts, cuts[1:]):
            piece = swap(others[step - 1][:, low:high], step)
            returned.append((piece, step, chunk * width + low))
    for piece, step, offset in returned:
        buffer = place(position, buffer, piece, step, offset)
    return buffer


def solution(mesh):
    in_specs = (
        P("member", "tile"),
        P("tile"),
        P("tile"),
        P("tile", None),
        P(("tile", "member"), None),
        P("member", "tile"),
    )
    out_specs = P("member", "tile")
    return jax.shard_map(
        on_device, mesh=mesh, in_specs=in_specs, out_specs=out_specs, check_vma=False
    )
```

```python
import functools

import jax
import jax.numpy as jnp
from jax import lax
from jax.experimental import pallas as pl
from jax.experimental.pallas import tpu as pltpu
from jax.sharding import PartitionSpec as P


LOC = 1024
NS_ITERS = 3
LANES = 128
WINDOW = 2 * LOC
CHUNKS = 2
BLOCK = 512


def partners(count, step):
    return [(i, i ^ step) for i in range(count)]


def swap(block, step):
    return lax.ppermute(block, "member", partners(lax.axis_size("member"), step))


def cut(position, state, step, chunk, count, part=(0, 1)):
    rows, total = state.shape
    width = total // (count * CHUNKS)
    low, high = int(part[0] * width), int(part[1] * width)
    start = ((position[0] ^ step) * CHUNKS + chunk) * width + low
    return lax.dynamic_slice(state, (0, start), (rows, high - low))


def lead_kernel(first, state_ref, out_ref, sem):
    start = pl.multiple_of(first(lax.axis_index("member")), LANES)
    copy = pltpu.make_async_copy(state_ref.at[:, pl.ds(start, out_ref.shape[1])], out_ref, sem)
    copy.start()
    copy.wait()


def lead_piece(state, step, width):
    rows, total = state.shape
    patch = total // lax.axis_size("member")
    return pl.pallas_call(
        functools.partial(lead_kernel, lambda pos: (pos ^ step) * patch),
        in_specs=[pl.BlockSpec(memory_space=pl.ANY)],
        out_specs=pl.BlockSpec(memory_space=pltpu.VMEM),
        scratch_shapes=[pltpu.SemaphoreType.DMA],
        out_shape=pltpu.VMEM((rows, width), state.dtype),
        cost_estimate=pl.CostEstimate(
            flops=0, transcendentals=0, bytes_accessed=2 * rows * width
        ),
    )(state)


def pick_kernel(pos_ref, start_ref, index_ref, own_ref, low_ref, high_ref, out_ref, pair_ref, pool):
    step = pl.program_id(0)
    own = own_ref.shape[1]
    span = WINDOW + LANES

    @pl.when(step == 0)
    def _():
        pool[:, :LOC] = low_ref[...]
        pool[:, LOC : LOC + own] = own_ref[...]
        pool[:, LOC + own :] = high_ref[...]

    start = pl.multiple_of(start_ref[pos_ref[0] ^ step], LANES)
    relative = index_ref[0] - start
    window = pool[:, pl.ds(start, span)]
    half = LOC // 4
    for part in range(4):
        where = relative[:, part * half : (part + 1) * half]
        hot = lax.broadcasted_iota(jnp.int32, (span, half), 0) == where
        hot = jnp.where(hot, 1.0, 0.0).astype(jnp.bfloat16)
        picked = jnp.dot(window, hot, preferred_element_type=jnp.float32)
        picked = picked.astype(jnp.bfloat16)
        out_ref[0, :, part * half : (part + 1) * half] = picked[: out_ref.shape[1]]

        @pl.when(step == 0)
        def _():
            pair_ref[:, part * half : (part + 1) * half] = picked[out_ref.shape[1] :]


def pick(position, starts, index, own, low, high, members):
    count = index.shape[0]
    rows, width = own.shape
    whole = lambda shape: pl.BlockSpec(shape, lambda i, pos, start: (0,) * len(shape))
    return pl.pallas_call(
        pick_kernel,
        grid_spec=pltpu.PrefetchScalarGridSpec(
            num_scalar_prefetch=2,
            grid=(count,),
            in_specs=[
                pl.BlockSpec((1, 1, LOC), lambda i, pos, start: (pos[0] ^ i, 0, 0)),
                whole(own.shape),
                whole(low.shape),
                whole(high.shape),
            ],
            out_specs=[
                pl.BlockSpec((1, members, LOC), lambda i, pos, start: (i, 0, 0)),
                whole((rows - members, LOC)),
            ],
            scratch_shapes=[pltpu.VMEM((rows, width + 2 * LOC), jnp.bfloat16)],
        ),
        compiler_params=pltpu.CompilerParams(vmem_limit_bytes=20 << 20),
        out_shape=[
            jax.ShapeDtypeStruct((count, members, LOC), jnp.bfloat16),
            jax.ShapeDtypeStruct((rows - members, LOC), jnp.bfloat16),
        ],
        cost_estimate=pl.CostEstimate(
            flops=2 * count * rows * (WINDOW + LANES) * LOC,
            transcendentals=0,
            bytes_accessed=2 * rows * width + 2 * count * rows * LOC,
        ),
    )(position, starts, index.reshape(count, 1, LOC), own, low, high)


def update_kernel(count, aliased, pos_ref, transform_ref, *refs):
    blocks = refs[:count]
    outs = refs[count + aliased : 2 * count + aliased]
    pert = refs[-1]
    rows = blocks[0].shape[0]
    values = [block[...].astype(jnp.float32) for block in blocks]
    total = jnp.sum(values[0], axis=0, keepdims=True)
    for value in values[1:]:
        total += jnp.sum(value, axis=0, keepdims=True)
    mean = total / (count * rows)
    for k, value in enumerate(values):
        pert[k * rows : (k + 1) * rows, :] = (value - mean).astype(jnp.bfloat16)
    combined = jnp.dot(transform_ref[...], pert[...], preferred_element_type=jnp.float32)
    result = (mean + combined).astype(jnp.bfloat16)
    for k in range(count):
        outs[k][...] = result[k * rows : (k + 1) * rows]


def update_state(position, transform, state, received, chunk, buffer):
    rows, total = state.shape
    count = len(received) + 1
    members = transform.shape[0]
    width = received[0].shape[1]
    block = min(BLOCK, width)
    per = width // block
    own = pl.BlockSpec((rows, block), lambda i, pos: (0, (pos[0] * CHUNKS + chunk) * per + i))
    plain = pl.BlockSpec((rows, block), lambda i, pos: (0, i))
    aliased = 0 if buffer is None else 1
    extra = [] if buffer is None else [pl.BlockSpec(memory_space=pl.ANY)]
    return pl.pallas_call(
        functools.partial(update_kernel, count, aliased),
        grid_spec=pltpu.PrefetchScalarGridSpec(
            num_scalar_prefetch=1,
            grid=(per,),
            in_specs=[pl.BlockSpec((members, members), lambda i, pos: (0, 0)), own]
            + [plain] * (count - 1)
            + extra,
            out_specs=[own] + [plain] * (count - 1),
            scratch_shapes=[pltpu.VMEM((members, block), jnp.bfloat16)],
        ),
        out_shape=[jax.ShapeDtypeStruct((rows, total), state.dtype)]
        + [jax.ShapeDtypeStruct((rows, width), state.dtype)] * (count - 1),
        input_output_aliases={} if buffer is None else {2 + count: 0},
        compiler_params=pltpu.CompilerParams(vmem_limit_bytes=16 << 20),
        cost_estimate=pl.CostEstimate(
            flops=2 * members * members * width,
            transcendentals=0,
            bytes_accessed=4 * members * width + 2 * members * members,
        ),
    )(position, transform, state, *received, *([] if buffer is None else [buffer]))


def place_kernel(first, piece_ref, buffer_ref, out_ref, sem):
    width = piece_ref.shape[1]
    start = pl.multiple_of(first(lax.axis_index("member")), LANES)
    copy = pltpu.make_async_copy(piece_ref, out_ref.at[:, pl.ds(start, width)], sem)
    copy.start()
    copy.wait()


def place(buffer, piece, step, offset):
    rows, width = piece.shape
    patch = buffer.shape[1] // lax.axis_size("member")
    return pl.pallas_call(
        functools.partial(place_kernel, lambda pos: (pos ^ step) * patch + offset),
        in_specs=[pl.BlockSpec(memory_space=pl.ANY)] * 2,
        out_specs=pl.BlockSpec(memory_space=pl.ANY),
        scratch_shapes=[pltpu.SemaphoreType.DMA],
        compiler_params=pltpu.CompilerParams(vmem_limit_bytes=1 << 20),
        out_shape=jax.ShapeDtypeStruct(buffer.shape, buffer.dtype),
        input_output_aliases={1: 0},
        cost_estimate=pl.CostEstimate(
            flops=0, transcendentals=0, bytes_accessed=2 * rows * width
        ),
    )(piece, buffer)


def product(left, right, dims):
    return lax.dot_general(left, right, (dims, ((), ())), preferred_element_type=jnp.float32)


def analysis(obs_block, obs_pair, loc_row):
    members = obs_block.shape[0]
    block_f = obs_block.astype(jnp.float32)
    obs_mean = jnp.mean(block_f, axis=0)
    obs_root = jnp.sqrt(obs_pair[1].astype(jnp.float32) * loc_row)
    scaled = ((block_f - obs_mean) * obs_root).astype(jnp.bfloat16)
    innovation = (obs_pair[0].astype(jnp.float32) - obs_mean) * obs_root
    gram_matrix = product(scaled, scaled, ((1,), (1,)))
    identity = jnp.eye(members, dtype=jnp.float32)
    system = gram_matrix + (members - 1.0) * identity
    projection = jnp.dot(scaled.astype(jnp.float32), innovation, precision=lax.Precision.HIGHEST)
    norm_a = jnp.sqrt(jnp.sum(system * system))
    upper_iter = system / norm_a
    lower_iter = identity
    for sweep in range(NS_ITERS):
        upper_b = upper_iter.astype(jnp.bfloat16)
        lower_b = lower_iter.astype(jnp.bfloat16)
        half_step = (1.5 * identity - 0.5 * product(lower_b, upper_b, ((1,), (0,)))).astype(
            jnp.bfloat16
        )
        if sweep + 1 < NS_ITERS:
            upper_iter = product(upper_b, half_step, ((1,), (0,)))
        lower_iter = product(half_step, lower_b, ((1,), (0,)))
    invroot = lower_iter / jnp.sqrt(norm_a)
    inner_w = jnp.dot(invroot, projection, precision=lax.Precision.HIGHEST)
    mean_w = jnp.dot(invroot, inner_w, precision=lax.Precision.HIGHEST)
    transform = jnp.sqrt(members - 1.0) * invroot + mean_w[:, None]
    return transform.astype(jnp.bfloat16).T


def shift_tiles(block, step):
    count = lax.axis_size("tile")
    return lax.ppermute(block, "tile", [(i, (i + step) % count) for i in range(count)])


def send_order(count):
    return [count - 1, *range(1, count - 1)]


def on_device(hx, obs_value, obs_rinv, obs_index, loc_weight, state):
    rows = hx.shape[0]
    count = lax.axis_size("member")
    position = lax.axis_index("member").astype(jnp.int32).reshape(1)
    steps = send_order(count)

    source = state

    def send(chunk, step, part=(0, 1)):
        nonlocal source
        piece = cut(position, source, step, chunk, count, part)
        source, piece = lax.optimization_barrier((source, piece))
        return swap(piece, step)

    def send_chunk(chunk, order):
        return {step: send(chunk, step) for step in order}

    piece = lead_piece(source, steps[0], state.shape[1] // (4 * count * CHUNKS))
    source, piece = lax.optimization_barrier((source, piece))
    head = swap(piece, steps[0])
    rest = send(0, steps[0], (0.25, 1))
    arrived = [send_chunk(0, steps[1:])]
    arrived[0][steps[0]] = jnp.concatenate([head, rest], axis=1)

    pad = jnp.zeros((14, hx.shape[1]), hx.dtype)
    stacked = jnp.concatenate([hx, obs_value[None], obs_rinv[None], pad], axis=0)
    low = shift_tiles(stacked[:, -LOC:], 1)
    high = shift_tiles(stacked[:, :LOC], -1)
    limit = hx.shape[1] - WINDOW + 2 * LOC - LANES
    starts = jnp.minimum(jnp.min(obs_index, axis=1) // LANES * LANES, limit)
    picked, obs_pair = pick(position, starts, obs_index, stacked, low, high, rows)
    others = {step: swap(picked[step], step) for step in steps}
    obs_block = jnp.concatenate([picked[0]] + [others[s] for s in range(1, count)], axis=0)

    for chunk in range(1, CHUNKS):
        arrived.append(send_chunk(chunk, steps))

    transform = analysis(obs_block, obs_pair, loc_weight[0])

    buffer, returned = None, []
    back = steps[:0:-1] + steps[:1]
    width = state.shape[1] // (count * CHUNKS)
    for chunk in range(CHUNKS):
        received = [arrived[chunk][step] for step in range(1, count)]
        buffer, *others = update_state(position, transform, state, received, chunk, buffer)
        last = chunk == CHUNKS - 1
        for step in back[:-1]:
            returned.append((swap(others[step - 1], step), step, chunk * width))
        step, cuts = back[-1], [0, width]
        if last:
            cuts = [0, width * 3 // 4, width]
        for low, high in zip(cuts, cuts[1:]):
            piece = swap(others[step - 1][:, low:high], step)
            returned.append((piece, step, chunk * width + low))
    for piece, step, offset in returned:
        buffer = place(buffer, piece, step, offset)
    return buffer


def solution(mesh):
    in_specs = (
        P("member", "tile"),
        P("tile"),
        P("tile"),
        P("tile", None),
        P(("tile", "member"), None),
        P("member", "tile"),
    )
    out_specs = P("member", "tile")
    return jax.shard_map(
        on_device, mesh=mesh, in_specs=in_specs, out_specs=out_specs, check_vma=False
    )
```

```python
import functools

import jax
import jax.numpy as jnp
from jax import lax
from jax.experimental import pallas as pl
from jax.experimental.pallas import tpu as pltpu
from jax.sharding import PartitionSpec as P


LOC = 1024
NS_ITERS = 3
LANES = 128
WINDOW = 2 * LOC
CHUNKS = 2
BLOCK = 1024


def partners(count, step):
    return [(i, i ^ step) for i in range(count)]


def swap(block, step):
    return lax.ppermute(block, "member", partners(lax.axis_size("member"), step))


def cut(position, state, step, chunk, count, part=(0, 1)):
    rows, total = state.shape
    width = total // (count * CHUNKS)
    low, high = int(part[0] * width), int(part[1] * width)
    start = ((position[0] ^ step) * CHUNKS + chunk) * width + low
    return lax.dynamic_slice(state, (0, start), (rows, high - low))


def pick_kernel(pos_ref, start_ref, index_ref, own_ref, low_ref, high_ref, out_ref, pair_ref, pool):
    step = pl.program_id(0)
    own = own_ref.shape[1]
    span = WINDOW + LANES

    @pl.when(step == 0)
    def _():
        pool[:, :LOC] = low_ref[...]
        pool[:, LOC : LOC + own] = own_ref[...]
        pool[:, LOC + own :] = high_ref[...]

    start = pl.multiple_of(start_ref[pos_ref[0] ^ step], LANES)
    relative = index_ref[0] - start
    window = pool[:, pl.ds(start, span)]
    half = LOC // 4
    for part in range(4):
        where = relative[:, part * half : (part + 1) * half]
        hot = lax.broadcasted_iota(jnp.int32, (span, half), 0) == where
        hot = jnp.where(hot, 1.0, 0.0).astype(jnp.bfloat16)
        picked = jnp.dot(window, hot, preferred_element_type=jnp.float32)
        picked = picked.astype(jnp.bfloat16)
        out_ref[0, :, part * half : (part + 1) * half] = picked[: out_ref.shape[1]]

        @pl.when(step == 0)
        def _():
            pair_ref[:, part * half : (part + 1) * half] = picked[out_ref.shape[1] :]


def pick(position, starts, index, own, low, high, members):
    count = index.shape[0]
    rows, width = own.shape
    whole = lambda shape: pl.BlockSpec(shape, lambda i, pos, start: (0,) * len(shape))
    return pl.pallas_call(
        pick_kernel,
        grid_spec=pltpu.PrefetchScalarGridSpec(
            num_scalar_prefetch=2,
            grid=(count,),
            in_specs=[
                pl.BlockSpec((1, 1, LOC), lambda i, pos, start: (pos[0] ^ i, 0, 0)),
                whole(own.shape),
                whole(low.shape),
                whole(high.shape),
            ],
            out_specs=[
                pl.BlockSpec((1, members, LOC), lambda i, pos, start: (i, 0, 0)),
                whole((rows - members, LOC)),
            ],
            scratch_shapes=[pltpu.VMEM((rows, width + 2 * LOC), jnp.bfloat16)],
        ),
        compiler_params=pltpu.CompilerParams(vmem_limit_bytes=20 << 20),
        out_shape=[
            jax.ShapeDtypeStruct((count, members, LOC), jnp.bfloat16),
            jax.ShapeDtypeStruct((rows - members, LOC), jnp.bfloat16),
        ],
        cost_estimate=pl.CostEstimate(
            flops=2 * count * rows * (WINDOW + LANES) * LOC,
            transcendentals=0,
            bytes_accessed=2 * rows * width + 2 * count * rows * LOC,
        ),
    )(position, starts, index.reshape(count, 1, LOC), own, low, high)


def update_kernel(count, aliased, pos_ref, transform_ref, *refs):
    blocks = refs[:count]
    outs = refs[count + aliased : 2 * count + aliased]
    pert = refs[-1]
    rows = blocks[0].shape[0]
    values = [block[...].astype(jnp.float32) for block in blocks]
    total = jnp.sum(values[0], axis=0, keepdims=True)
    for value in values[1:]:
        total += jnp.sum(value, axis=0, keepdims=True)
    mean = total / (count * rows)
    for k, value in enumerate(values):
        pert[k * rows : (k + 1) * rows, :] = (value - mean).astype(jnp.bfloat16)
    combined = jnp.dot(transform_ref[...], pert[...], preferred_element_type=jnp.float32)
    result = (mean + combined).astype(jnp.bfloat16)
    for k in range(count):
        outs[k][...] = result[k * rows : (k + 1) * rows]


def update_state(position, transform, state, received, chunk, buffer):
    rows, total = state.shape
    count = len(received) + 1
    members = transform.shape[0]
    width = received[0].shape[1]
    block = min(BLOCK, width)
    per = width // block
    own = pl.BlockSpec((rows, block), lambda i, pos: (0, (pos[0] * CHUNKS + chunk) * per + i))
    plain = pl.BlockSpec((rows, block), lambda i, pos: (0, i))
    aliased = 0 if buffer is None else 1
    extra = [] if buffer is None else [pl.BlockSpec(memory_space=pl.ANY)]
    return pl.pallas_call(
        functools.partial(update_kernel, count, aliased),
        grid_spec=pltpu.PrefetchScalarGridSpec(
            num_scalar_prefetch=1,
            grid=(per,),
            in_specs=[pl.BlockSpec((members, members), lambda i, pos: (0, 0)), own]
            + [plain] * (count - 1)
            + extra,
            out_specs=[own] + [plain] * (count - 1),
            scratch_shapes=[pltpu.VMEM((members, block), jnp.bfloat16)],
        ),
        out_shape=[jax.ShapeDtypeStruct((rows, total), state.dtype)]
        + [jax.ShapeDtypeStruct((rows, width), state.dtype)] * (count - 1),
        input_output_aliases={} if buffer is None else {2 + count: 0},
        compiler_params=pltpu.CompilerParams(vmem_limit_bytes=16 << 20),
        cost_estimate=pl.CostEstimate(
            flops=2 * members * members * width,
            transcendentals=0,
            bytes_accessed=4 * members * width + 2 * members * members,
        ),
    )(position, transform, state, *received, *([] if buffer is None else [buffer]))


def place_kernel(first, pos_ref, piece_ref, buffer_ref, out_ref, sem):
    width = piece_ref.shape[1]
    start = pl.multiple_of(first(pos_ref[0]), LANES)
    copy = pltpu.make_async_copy(piece_ref, out_ref.at[:, pl.ds(start, width)], sem)
    copy.start()
    copy.wait()


def place(position, buffer, piece, step, offset):
    rows, width = piece.shape
    patch = buffer.shape[1] // lax.axis_size("member")
    return pl.pallas_call(
        functools.partial(place_kernel, lambda pos: (pos ^ step) * patch + offset),
        in_specs=[
            pl.BlockSpec(memory_space=pltpu.SMEM),
            pl.BlockSpec(memory_space=pl.ANY),
            pl.BlockSpec(memory_space=pl.ANY),
        ],
        out_specs=pl.BlockSpec(memory_space=pl.ANY),
        scratch_shapes=[pltpu.SemaphoreType.DMA],
        compiler_params=pltpu.CompilerParams(vmem_limit_bytes=1 << 20),
        out_shape=jax.ShapeDtypeStruct(buffer.shape, buffer.dtype),
        input_output_aliases={2: 0},
        cost_estimate=pl.CostEstimate(
            flops=0, transcendentals=0, bytes_accessed=2 * rows * width
        ),
    )(position, piece, buffer)


def product(left, right, dims):
    return lax.dot_general(left, right, (dims, ((), ())), preferred_element_type=jnp.float32)


def analysis(obs_block, obs_pair, loc_row):
    members = obs_block.shape[0]
    block_f = obs_block.astype(jnp.float32)
    obs_mean = jnp.mean(block_f, axis=0)
    obs_root = jnp.sqrt(obs_pair[1].astype(jnp.float32) * loc_row)
    scaled = ((block_f - obs_mean) * obs_root).astype(jnp.bfloat16)
    innovation = (obs_pair[0].astype(jnp.float32) - obs_mean) * obs_root
    gram_matrix = product(scaled, scaled, ((1,), (1,)))
    identity = jnp.eye(members, dtype=jnp.float32)
    system = gram_matrix + (members - 1.0) * identity
    projection = jnp.dot(scaled.astype(jnp.float32), innovation, precision=lax.Precision.HIGHEST)
    norm_a = jnp.sqrt(jnp.sum(system * system))
    upper_iter = system / norm_a
    lower_iter = identity
    for sweep in range(NS_ITERS):
        upper_b = upper_iter.astype(jnp.bfloat16)
        lower_b = lower_iter.astype(jnp.bfloat16)
        half_step = (1.5 * identity - 0.5 * product(lower_b, upper_b, ((1,), (0,)))).astype(
            jnp.bfloat16
        )
        if sweep + 1 < NS_ITERS:
            upper_iter = product(upper_b, half_step, ((1,), (0,)))
        lower_iter = product(half_step, lower_b, ((1,), (0,)))
    invroot = lower_iter / jnp.sqrt(norm_a)
    inner_w = jnp.dot(invroot, projection, precision=lax.Precision.HIGHEST)
    mean_w = jnp.dot(invroot, inner_w, precision=lax.Precision.HIGHEST)
    transform = jnp.sqrt(members - 1.0) * invroot + mean_w[:, None]
    return transform.astype(jnp.bfloat16).T


def shift_tiles(block, step):
    count = lax.axis_size("tile")
    return lax.ppermute(block, "tile", [(i, (i + step) % count) for i in range(count)])


def send_order(count):
    return [count - 1, *range(1, count - 1)]


def on_device(hx, obs_value, obs_rinv, obs_index, loc_weight, state):
    rows = hx.shape[0]
    count = lax.axis_size("member")
    position = lax.axis_index("member").astype(jnp.int32).reshape(1)
    steps = send_order(count)

    source = state

    def send(chunk, step, part=(0, 1)):
        nonlocal source
        piece = cut(position, source, step, chunk, count, part)
        source, piece = lax.optimization_barrier((source, piece))
        return swap(piece, step)

    def send_chunk(chunk, order):
        return {step: send(chunk, step) for step in order}

    head = send(0, steps[0], (0, 0.25))
    rest = send(0, steps[0], (0.25, 1))
    arrived = [send_chunk(0, steps[1:])]
    arrived[0][steps[0]] = jnp.concatenate([head, rest], axis=1)

    pad = jnp.zeros((14, hx.shape[1]), hx.dtype)
    stacked = jnp.concatenate([hx, obs_value[None], obs_rinv[None], pad], axis=0)
    low = shift_tiles(stacked[:, -LOC:], 1)
    high = shift_tiles(stacked[:, :LOC], -1)
    limit = hx.shape[1] - WINDOW + 2 * LOC - LANES
    starts = jnp.minimum(jnp.min(obs_index, axis=1) // LANES * LANES, limit)
    picked, obs_pair = pick(position, starts, obs_index, stacked, low, high, rows)
    others = {step: swap(picked[step], step) for step in steps}
    obs_block = jnp.concatenate([picked[0]] + [others[s] for s in range(1, count)], axis=0)

    for chunk in range(1, CHUNKS):
        arrived.append(send_chunk(chunk, steps))

    transform = analysis(obs_block, obs_pair, loc_weight[0])

    buffer, returned = None, []
    back = steps[:0:-1] + steps[:1]
    width = state.shape[1] // (count * CHUNKS)
    for chunk in range(CHUNKS):
        received = [arrived[chunk][step] for step in range(1, count)]
        buffer, *others = update_state(position, transform, state, received, chunk, buffer)
        last = chunk == CHUNKS - 1
        for step in back[:-1]:
            returned.append((swap(others[step - 1], step), step, chunk * width))
        step, cuts = back[-1], [0, width]
        if last:
            cuts = [0, width * 3 // 4, width]
        for low, high in zip(cuts, cuts[1:]):
            piece = swap(others[step - 1][:, low:high], step)
            returned.append((piece, step, chunk * width + low))
    for piece, step, offset in returned:
        buffer = place(position, buffer, piece, step, offset)
    return buffer


def solution(mesh):
    in_specs = (
        P("member", "tile"),
        P("tile"),
        P("tile"),
        P("tile", None),
        P(("tile", "member"), None),
        P("member", "tile"),
    )
    out_specs = P("member", "tile")
    return jax.shard_map(
        on_device, mesh=mesh, in_specs=in_specs, out_specs=out_specs, check_vma=False
    )
```
